768 devices in a mesh: grp: 24 (over z, y_lo), head: 32 (over y_hi, x, core).
Axes of the slice: x: 4, y: 8 (y_hi: 4, y_lo: 2; y = y_hi * 2 + y_lo), z: 12, core: 2. Of those that a mesh axis runs over, the one named last changes fastest.
Arguments:
- queries: bfloat16 [32, 48, 4096], P('head'), may hold values from -1500 to 1500
- shared_prefix_keys: bfloat16 [32, 3072, 512], P('head', 'grp'), may hold values from -6 to 6
- shared_prefix_values: bfloat16 [32, 3072, 512], P('head', 'grp'), may hold values from -6 to 6
- row_suffix_keys: bfloat16 [32, 48, 16, 512], P('head', 'grp'), may hold values from -6 to 6
- row_suffix_values: bfloat16 [32, 48, 16, 512], P('head', 'grp'), may hold values from -6 to 6
- suffix_lengths: int32 [32, 48], P('head', 'grp'), may hold values from 1 to 16, as said below
- residual: bfloat16 [32, 48, 2048], P('head', 'grp'), may hold values from -4 to 4
- out_weight: bfloat16 [4096, 2048], P('head'), may hold values from -0.5 to 0.5
- norm_gain: float32 [2048], replicated, may hold values from 0.5 to 2
- router_weight: bfloat16 [2048, 64], replicated, may hold values from -0.125 to 0.125
- gate_weights: bfloat16 [64, 2048, 384], P('head'), may hold values from -0.125 to 0.125
- up_weights: bfloat16 [64, 2048, 384], P('head'), may hold values from -0.125 to 0.125
- down_weights: bfloat16 [64, 384, 2048], P('head'), may hold values from -0.3125 to 0.3125
- expert_ids: int32 [32, 48, 8], P('head', 'grp'), may hold values from 0 to 63, all different within a row; in each aligned block of 2 rows (0 to 1, 2 to 3, ..., all dimensions but the last counted through in order) at most 2 rows name the same one
Outputs:
- layer_out: float32 [32, 48, 2048], P('head', 'grp')
The draws below stay inside these ranges and needn't reach their ends.
Inputs may be any that keep to these rules, and one draw needn't show every extreme that they name: `expert_ids`: each row names 8 different experts; in each aligned block of 2 rows (the rows of one device, prompts then rows in order) no expert is named by more than 2 rows, a bound that some block reaches. `suffix_lengths`: every prompt has a row whose suffix holds 16 tokens.
All inputs are finite; a program needn't handle non-finite values.
Results may differ from the reference program's by a relative error of at most 0.007.
Values may be sent and summed in bfloat16 or wider, within the bound.
No kernel may reach another device: no remote copies, remote signals or barrier semaphores. Data moves between devices by JAX's collectives and lax.ppermute only.
A program may use at most 128 MiB of HBM per device.

```python
import math
import jax
import jax.numpy as jnp
import numpy as np
from jax import lax

D = 2048
QUERY_HEADS = 32
KEY_VALUE_HEADS = 4
HEAD_SIZE = 128
FF = 384
EXPERTS = 64
TOPK = 8
SUFFIX_MAXIMUM = 16
ROW_DEV = 2
CAP = 2
PREFIX_LENGTH = 3072
PROMPT_ROWS = 48
PROMPT_COUNT = 32


def draw_pair(key):
    key_portion = jax.random.fold_in(key, 101)
    query_part = jax.random.fold_in(key, 202)
    scale_part = jax.random.fold_in(key, 404)
    rows_of_keys = jnp.clip(jax.random.normal(key_portion, (PROMPT_COUNT, PREFIX_LENGTH, KEY_VALUE_HEADS * HEAD_SIZE), jnp.float32), -6.0, 6.0)
    base_queries = jnp.clip(jax.random.normal(query_part, (PROMPT_COUNT, PROMPT_ROWS, QUERY_HEADS, HEAD_SIZE), jnp.float32), -6.0, 6.0)
    head_scale = jnp.exp(jax.random.uniform(scale_part, (PROMPT_COUNT, PROMPT_ROWS, QUERY_HEADS, 1), jnp.float32, math.log(0.5), math.log(16.0)))
    query_rows = (base_queries * head_scale).reshape(PROMPT_COUNT, PROMPT_ROWS, QUERY_HEADS * HEAD_SIZE)
    return (rows_of_keys, query_rows)


def draw_queries(key, part):
    return draw_pair(key)[1].astype(jnp.bfloat16)


def draw_shared_prefix_keys(key, part):
    return draw_pair(key)[0].astype(jnp.bfloat16)


def draw_suffix_lengths(key, part):
    base_lengths = jax.random.randint(jax.random.fold_in(key, 7), (PROMPT_COUNT, PROMPT_ROWS), 1, SUFFIX_MAXIMUM + 1)
    long_row = jax.random.randint(jax.random.fold_in(key, 8), (PROMPT_COUNT,), 0, PROMPT_ROWS)
    is_long = jnp.arange(PROMPT_ROWS)[None, :] == long_row[:, None]
    return jnp.where(is_long, SUFFIX_MAXIMUM, base_lengths).astype(jnp.int32)


def level_of(key, dims, pieces, low, largest):
    level, own = 1.0, jax.random.fold_in(key, 6)
    for position, blocks in pieces:
        draws = jnp.exp(jax.random.uniform(jax.random.fold_in(own, position), (blocks,), jnp.float32, low / len(pieces), largest / len(pieces)))
        level = level * jnp.repeat(draws, dims[position] // blocks).reshape([-1 if axis == position else 1 for axis in range(len(dims))])
    return level


def deal_out(key, own, number, rows, number_of, top, reach, slope):
    sequence = jax.random.permutation(key, number_of)
    heavy_load, common = load_shares(number_of, rows * top, reach, slope, True), load_shares(number_of, rows * top, reach, slope, False)
    places = jnp.arange(number_of)

    def named(lengths, turn):
        used = int((lengths > 0).sum())
        fixed = max(1, used // 4)
        passed = fixed + (places - fixed + turn * (used - fixed)) % max(1, number_of - fixed)
        return jnp.zeros((number_of,), jnp.int32).at[sequence[jnp.where(places < fixed, places, passed)]].set(jnp.asarray(lengths, jnp.int32))

    lengths = jnp.where(number % 4 == 0, named(heavy_load, number // 4), named(common, number - number // 4 - 1))
    mixed = jax.random.permutation(jax.random.fold_in(own, 3), number_of)
    source_of, sink = mixed[0:number_of // 2 * 2:2], mixed[1:number_of // 2 * 2:2]
    room = jnp.minimum(lengths[source_of] - 1, reach - lengths[sink]) // 2
    room = jnp.where((source_of == sequence[0]) | (sink == sequence[0]) | (lengths[sink] == 0), 0, jnp.maximum(room, 0))
    passed = jax.random.randint(jax.random.fold_in(own, 4), (number_of // 2,), 0, 1 << 20) % (room + 1)
    lengths = lengths.at[source_of].add(-passed).at[sink].add(passed)
    labels = jnp.searchsorted(jnp.cumsum(lengths), jnp.arange(rows * top), side="right").astype(jnp.int32)
    listing = labels.reshape(top, rows).T
    listing = listing[jax.random.permutation(jax.random.fold_in(own, 1), rows)]
    turn = jax.random.randint(jax.random.fold_in(own, 2), (rows, 1), 0, top)
    return jnp.take_along_axis(listing, (jnp.arange(top)[None, :] + turn) % top, axis=1)


def load_shares(number_of, total, limit, lean, full):
    portions = [(1 << 20) // math.isqrt(rank ** lean) + 1 for rank in range(1, number_of + 1)]
    largest = limit if full else min(limit, max(-(-total // number_of), total * portions[0] // sum(portions)))
    least = 1 if total - largest >= number_of - 1 else 0
    holding, spare = [largest] + [least] * (number_of - 1), total - largest - least * (number_of - 1)
    while spare > 0:
        movable = [i for i in range(1, number_of) if holding[i] < largest] or [i for i in range(1, number_of) if holding[i] < limit]
        mass, remaining = sum([portions[i] for i in movable]), spare
        for i in movable:
            more = min(limit - holding[i], max(1, remaining * portions[i] // mass), spare)
            holding[i] = holding[i] + more
            spare = spare - more
    return np.array(holding)


def bell_draw(rng, shape, scale, reach, pieces=(), held_as=jnp.bfloat16):
    entries = jax.random.normal(rng, shape, jnp.float32) * scale
    if len(pieces) > 0:
        entries = level_of(rng, shape, pieces, -0.22, 0.18) * entries
    return jnp.clip(entries, min=-reach, max=reach).astype(held_as)


def setup_inputs(seed: int = 0) -> dict:
    arg_keys = jax.random.split(jax.random.key(seed), 15)
    queries = draw_queries(jax.random.fold_in(arg_keys[14], 71), 0)
    shared_prefix_keys = draw_shared_prefix_keys(jax.random.fold_in(arg_keys[14], 71), 0)
    shared_prefix_values = bell_draw(arg_keys[2], (PROMPT_COUNT, PREFIX_LENGTH, KEY_VALUE_HEADS * HEAD_SIZE), 1.0, 6.0, ((0, 32), (1, 24)))
    row_suffix_keys = bell_draw(arg_keys[3], (PROMPT_COUNT, PROMPT_ROWS, SUFFIX_MAXIMUM, KEY_VALUE_HEADS * HEAD_SIZE), 1.0, 6.0, ((0, 32), (1, 24)))
    row_suffix_values = bell_draw(arg_keys[4], (PROMPT_COUNT, PROMPT_ROWS, SUFFIX_MAXIMUM, KEY_VALUE_HEADS * HEAD_SIZE), 1.0, 6.0, ((0, 32), (1, 24)))
    suffix_lengths = draw_suffix_lengths(jax.random.fold_in(arg_keys[14], 71), 0)
    residual = bell_draw(arg_keys[6], (PROMPT_COUNT, PROMPT_ROWS, D), 0.5, 4.0, ((0, 32), (1, 24)))
    out_weight = bell_draw(arg_keys[7], (QUERY_HEADS * HEAD_SIZE, D), HEAD_SIZE ** -0.5, 0.5, ((0, 32),))
    norm_gain = jnp.clip(jnp.exp(jax.random.uniform(arg_keys[8], (D,), jnp.float32, math.log(0.5), math.log(2.0))), 0.5, 2.0)
    router_weight = bell_draw(arg_keys[9], (D, EXPERTS), D ** -0.5, 0.125)
    gate_weights = bell_draw(arg_keys[10], (EXPERTS, D, FF), D ** -0.5, 0.125, ((0, 32),))
    up_weights = bell_draw(arg_keys[11], (EXPERTS, D, FF), D ** -0.5, 0.125, ((0, 32),))
    down_weights = bell_draw(arg_keys[12], (EXPERTS, FF, D), FF ** -0.5, 0.3125, ((0, 32),))
    expert_ids_keys = jax.random.split(jax.random.fold_in(arg_keys[13], 1), PROMPT_COUNT * PROMPT_ROWS // ROW_DEV)
    expert_ids_turns = jax.random.permutation(jax.random.fold_in(arg_keys[13], 3), PROMPT_COUNT * PROMPT_ROWS // ROW_DEV)
    expert_ids = jax.vmap(lambda own, number: deal_out(jax.random.fold_in(arg_keys[13], 2), own, number, ROW_DEV, EXPERTS, TOPK, CAP, 2))(expert_ids_keys, expert_ids_turns).reshape((PROMPT_COUNT, PROMPT_ROWS, TOPK))
    return {"queries": queries, "shared_prefix_keys": shared_prefix_keys, "shared_prefix_values": shared_prefix_values, "row_suffix_keys": row_suffix_keys, "row_suffix_values": row_suffix_values, "suffix_lengths": suffix_lengths, "residual": residual, "out_weight": out_weight, "norm_gain": norm_gain, "router_weight": router_weight, "gate_weights": gate_weights, "up_weights": up_weights, "down_weights": down_weights, "expert_ids": expert_ids}


masked_score = -1e+30
norm_epsilon = 1e-06

def reference(queries, shared_prefix_keys, shared_prefix_values, row_suffix_keys, row_suffix_values, suffix_lengths, residual, out_weight, norm_gain, router_weight, gate_weights, up_weights, down_weights, expert_ids):
    query_group_width = QUERY_HEADS // KEY_VALUE_HEADS
    score_scale = 1.0 / math.sqrt(HEAD_SIZE)

    def one_prompt(prompt_parts):
        query_tile, key_tile, value_tile, suffix_key_rows, suffix_value_rows, row_lengths = prompt_parts
        heads_of_queries = query_tile.astype(jnp.float32).reshape(PROMPT_ROWS, KEY_VALUE_HEADS, query_group_width, HEAD_SIZE)
        heads_of_keys = key_tile.astype(jnp.float32).reshape(PREFIX_LENGTH, KEY_VALUE_HEADS, HEAD_SIZE)
        heads_of_values = value_tile.astype(jnp.float32).reshape(PREFIX_LENGTH, KEY_VALUE_HEADS, HEAD_SIZE)
        suffix_key_heads = suffix_key_rows.astype(jnp.float32).reshape(PROMPT_ROWS, SUFFIX_MAXIMUM, KEY_VALUE_HEADS, HEAD_SIZE)
        suffix_value_heads = suffix_value_rows.astype(jnp.float32).reshape(PROMPT_ROWS, SUFFIX_MAXIMUM, KEY_VALUE_HEADS, HEAD_SIZE)
        pre_scores = jnp.einsum('rkgd,pkd->rkgp', heads_of_queries, heads_of_keys) * score_scale
        in_suffix = (jnp.arange(SUFFIX_MAXIMUM)[None, :] < row_lengths[:, None])[:, None, None, :]
        suf_scores = jnp.einsum('rkgd,rskd->rkgs', heads_of_queries, suffix_key_heads) * score_scale
        suf_scores = jnp.where(in_suffix, suf_scores, masked_score)
        top_score = jnp.maximum(lax.optimization_barrier(jnp.max(pre_scores, -1)), lax.optimization_barrier(jnp.max(suf_scores, -1)))
        pre_terms = jnp.exp(pre_scores - top_score[..., None])
        suf_terms = jnp.where(in_suffix, jnp.exp(suf_scores - top_score[..., None]), 0.0)
        total_mass = lax.optimization_barrier(jnp.sum(pre_terms, -1)) + lax.optimization_barrier(jnp.sum(suf_terms, -1))
        pre_round = lax.optimization_barrier(pre_terms.astype(jnp.bfloat16)).astype(jnp.float32)
        suf_round = lax.optimization_barrier(suf_terms.astype(jnp.bfloat16)).astype(jnp.float32)
        weighted = jnp.einsum('rkgp,pkd->rkgd', pre_round, heads_of_values) + jnp.einsum('rkgs,rskd->rkgd', suf_round, suffix_value_heads)
        return (weighted / total_mass[..., None]).reshape(PROMPT_ROWS, QUERY_HEADS * HEAD_SIZE).astype(jnp.bfloat16)
    attention = lax.map(one_prompt, (queries, shared_prefix_keys, shared_prefix_values, row_suffix_keys, row_suffix_values, suffix_lengths))
    row_total = PROMPT_COUNT * PROMPT_ROWS
    flat_attn = attention.reshape(row_total, QUERY_HEADS * HEAD_SIZE)
    projected = jnp.dot(flat_attn, out_weight, preferred_element_type=jnp.float32)
    hidden_state = residual.reshape(row_total, D).astype(jnp.float32) + projected
    mean_square = lax.optimization_barrier(jnp.mean(hidden_state * hidden_state, -1, keepdims=True))
    normed = (hidden_state * lax.rsqrt(mean_square + norm_epsilon) * norm_gain).astype(jnp.bfloat16)
    logits = jnp.dot(normed, router_weight, preferred_element_type=jnp.float32)
    chosen_ids = expert_ids.reshape(row_total, TOPK)
    chosen_logits = jnp.take_along_axis(logits, chosen_ids, 1)
    expo_terms = jnp.exp(chosen_logits)
    route_weights = expo_terms / lax.optimization_barrier(jnp.sum(expo_terms, -1, keepdims=True))
    block_count = row_total // ROW_DEV
    per_block = ROW_DEV * TOPK
    assigned = chosen_ids.reshape(block_count, per_block)
    one_hot = (assigned[..., None] == jnp.arange(EXPERTS, dtype=jnp.int32)).astype(jnp.int32)
    earlier = jnp.cumsum(one_hot, 1) - one_hot
    slot_index = lax.optimization_barrier(jnp.sum(earlier * one_hot, -1)).astype(jnp.int32)
    row_index = (jnp.arange(block_count, dtype=jnp.int32)[:, None] * ROW_DEV + jnp.arange(per_block, dtype=jnp.int32)[None, :] // TOPK).astype(jnp.int32)
    block_index = jnp.broadcast_to(jnp.arange(block_count, dtype=jnp.int32)[:, None], (block_count, per_block))
    row_table = jnp.full((EXPERTS, block_count, CAP), row_total, jnp.int32).at[assigned, block_index, slot_index].set(row_index)
    weight_table = jnp.zeros((EXPERTS, block_count, CAP), jnp.float32).at[assigned, block_index, slot_index].set(route_weights.reshape(block_count, per_block))
    padded = jnp.concatenate([normed, jnp.zeros((1, D), jnp.bfloat16)], 0)

    def expert_step(accumulated, expert_parts):
        row_slots, slot_weights, gate_matrix, up_matrix, down_matrix = expert_parts
        flat_slots = row_slots.reshape(-1)
        picked = padded[flat_slots]
        gate_out = jnp.dot(picked, gate_matrix, preferred_element_type=jnp.float32)
        up_out = jnp.dot(picked, up_matrix, preferred_element_type=jnp.float32)
        hidden_act = (jax.nn.silu(gate_out) * up_out).astype(jnp.bfloat16)
        expert_out = jnp.dot(hidden_act, down_matrix, preferred_element_type=jnp.float32).astype(jnp.bfloat16)
        expert_out = lax.optimization_barrier(expert_out).astype(jnp.float32)
        accumulated = accumulated.at[flat_slots].add(slot_weights.reshape(-1)[:, None] * expert_out)
        return (accumulated, None)
    accumulated, _ = lax.scan(expert_step, jnp.zeros((row_total + 1, D), jnp.float32), (row_table, weight_table, gate_weights, up_weights, down_weights))
    layer_out = hidden_state + accumulated[:row_total]
    return layer_out.reshape(PROMPT_COUNT, PROMPT_ROWS, D)
```

```python
import math

import jax
import jax.numpy as jnp
from jax import lax
from jax.sharding import PartitionSpec as P

QUERY_HEADS = 32
KEY_VALUE_HEADS = 4
HEAD_SIZE = 128
TOPK = 8
GROUP = QUERY_HEADS // KEY_VALUE_HEADS

masked_score = -1e30
norm_epsilon = 1e-06
f32 = jnp.float32
bf16 = jnp.bfloat16


def rounded(x):
    return lax.reduce_precision(x, 8, 7)


def two_pieces(x):
    high = rounded(x)
    return high, rounded(x - high)


def exchange(x, axis):
    return lax.all_to_all(x, axis, split_axis=0, concat_axis=0, tiled=True)


def shards(
    queries,
    shared_prefix_keys,
    shared_prefix_values,
    row_suffix_keys,
    row_suffix_values,
    suffix_lengths,
    residual,
    out_weight,
    norm_gain,
    router_weight,
    gate_weights,
    up_weights,
    down_weights,
    expert_ids,
):
    head_count = lax.axis_size("head")
    grp_count = lax.axis_size("grp")
    row_block = lax.axis_index("grp")
    every_row = queries.shape[1]
    own_rows = residual.shape[1]
    width = residual.shape[2]
    score_scale = 1.0 / math.sqrt(HEAD_SIZE)
    q = queries[0].reshape(every_row, KEY_VALUE_HEADS, GROUP, HEAD_SIZE)
    k = shared_prefix_keys[0].reshape(-1, KEY_VALUE_HEADS, HEAD_SIZE)
    v = shared_prefix_values[0].reshape(-1, KEY_VALUE_HEADS, HEAD_SIZE)
    scores = jnp.einsum("rkgd,pkd->rkgp", q, k, preferred_element_type=f32) * score_scale
    m_high, m_low = two_pieces(jnp.max(scores, -1))
    terms = jnp.exp(scores - (m_high + m_low)[..., None])
    s_high, s_low = two_pieces(jnp.sum(terms, -1))
    weighted = jnp.einsum("rkgp,pkd->rkgd", terms.astype(bf16), v, preferred_element_type=f32)
    values = weighted.astype(bf16).reshape(grp_count, own_rows * QUERY_HEADS, HEAD_SIZE)
    stats = jnp.stack([m_high, m_low, s_high, s_low]).astype(bf16)
    stats = stats.reshape(4, grp_count, own_rows * QUERY_HEADS).transpose(1, 0, 2)
    stats = jnp.pad(stats, ((0, 0), (0, 4), (0, HEAD_SIZE - own_rows * QUERY_HEADS)))
    arrived = exchange(jnp.concatenate([values, stats], 1), "grp")

    own_q = lax.dynamic_slice_in_dim(q, row_block * own_rows, own_rows, 0)
    suf_k = row_suffix_keys[0].reshape(own_rows, -1, KEY_VALUE_HEADS, HEAD_SIZE)
    suf_v = row_suffix_values[0].reshape(own_rows, -1, KEY_VALUE_HEADS, HEAD_SIZE)
    inside = (jnp.arange(suf_k.shape[1])[None, :] < suffix_lengths[0][:, None])[:, None, None, :]
    suf_scores = jnp.einsum("rkgd,rskd->rkgs", own_q, suf_k, preferred_element_type=f32)
    suf_scores = jnp.where(inside, suf_scores * score_scale, masked_score)
    suf_m = jnp.max(suf_scores, -1)
    suf_terms = jnp.where(inside, jnp.exp(suf_scores - suf_m[..., None]), 0.0)
    suf_s = jnp.sum(suf_terms, -1)
    suf_o = jnp.einsum(
        "rkgs,rskd->rkgd", suf_terms.astype(bf16), suf_v, preferred_element_type=f32
    )
    suf_m = suf_m.reshape(1, -1)
    suf_s = suf_s.reshape(1, -1)
    suf_o = suf_o.reshape(-1, HEAD_SIZE)

    n = own_rows * QUERY_HEADS
    parts = arrived[:, n : n + 4, :n].astype(f32)
    part_m = parts[:, 0] + parts[:, 1]
    part_s = parts[:, 2] + parts[:, 3]
    top = jnp.maximum(jnp.max(part_m, 0, keepdims=True), suf_m)
    scale = jnp.exp(part_m - top)
    suf_scale = jnp.exp(suf_m - top)
    mass = jnp.sum(scale * part_s, 0) + (suf_scale * suf_s)[0]
    total = jnp.sum(scale[..., None] * arrived[:, :n].astype(f32), 0) + suf_scale[0][:, None] * suf_o
    attn = (total / mass[:, None]).astype(bf16).reshape(own_rows, QUERY_HEADS, HEAD_SIZE)

    ids_row = jnp.pad(expert_ids[0].astype(bf16).reshape(1, 1, -1), ((0, 0), (0, 0), (0, HEAD_SIZE - own_rows * TOPK)))
    ids_row = jnp.broadcast_to(ids_row, (head_count, 1, HEAD_SIZE))
    arrived = exchange(jnp.concatenate([attn.transpose(1, 0, 2), ids_row], 1), "head")
    every_id = arrived[:, own_rows, : own_rows * TOPK].reshape(head_count * own_rows, TOPK)
    flat_attn = arrived[:, :own_rows].reshape(head_count * own_rows, HEAD_SIZE)
    partial = jnp.dot(flat_attn, out_weight, preferred_element_type=f32).astype(bf16)
    partial = exchange(partial.reshape(head_count, own_rows, width), "head")
    hidden = residual[0].astype(f32) + jnp.sum(partial.astype(f32), 0)
    mean_square = jnp.mean(hidden * hidden, -1, keepdims=True)
    normed = (hidden * lax.rsqrt(mean_square + norm_epsilon) * norm_gain).astype(bf16)

    x = exchange(jnp.broadcast_to(normed[None], (head_count, own_rows, width)), "head")
    x = x.reshape(head_count * own_rows, width)
    logits = jnp.dot(x, router_weight, preferred_element_type=f32)
    experts_all = router_weight.shape[1]
    local_experts = gate_weights.shape[0]
    expert_range = jnp.arange(experts_all, dtype=jnp.int32).astype(bf16)
    chosen = jnp.any(every_id[..., None] == expert_range, 1)
    expo = jnp.where(chosen, jnp.exp(logits), 0.0)
    route = expo / jnp.sum(expo, -1, keepdims=True)
    first = lax.axis_index("head") * local_experts
    own_route = lax.dynamic_slice_in_dim(route, first, local_experts, 1)
    gate_out = jnp.einsum("rd,edf->erf", x, gate_weights, preferred_element_type=f32)
    up_out = jnp.einsum("rd,edf->erf", x, up_weights, preferred_element_type=f32)
    act = (jax.nn.silu(gate_out) * up_out).astype(bf16)
    produced = jnp.einsum("erf,efd->erd", act, down_weights, preferred_element_type=f32)
    produced = produced.astype(bf16).astype(f32)
    mixed = jnp.sum(own_route.T[..., None] * produced, 0).astype(bf16)
    returned = exchange(mixed.reshape(head_count, own_rows, width), "head")
    return (hidden + jnp.sum(returned.astype(f32), 0))[None]


def solution(mesh):
    return jax.shard_map(
        shards,
        mesh=mesh,
        in_specs=(
            P("head", None, None),
            P("head", "grp", None),
            P("head", "grp", None),
            P("head", "grp", None, None),
            P("head", "grp", None, None),
            P("head", "grp"),
            P("head", "grp", None),
            P("head", None),
            P(),
            P(),
            P("head", None, None),
            P("head", None, None),
            P("head", None, None),
            P("head", "grp", None),
        ),
        out_specs=P("head", "grp", None),
        check_vma=False,
    )
```

```python
import math

import jax
import jax.numpy as jnp
from jax import lax
from jax.experimental import pallas as pl
from jax.experimental.pallas import tpu as pltpu
from jax.sharding import PartitionSpec as P

QUERY_HEADS = 32
KEY_VALUE_HEADS = 4
HEAD_SIZE = 128
GROUP = QUERY_HEADS // KEY_VALUE_HEADS
LANES = 128
STAT_ROWS = 16
DEST_ROWS = 8

masked_score = -1e30
norm_epsilon = 1e-06
score_scale = 1.0 / math.sqrt(HEAD_SIZE)
f32 = jnp.float32
bf16 = jnp.bfloat16
INTERPRET = False


def exchange(x, axis):
    return lax.all_to_all(x, axis, split_axis=0, concat_axis=0, tiled=True)


def kernel_call(body, outs, scratch, *args, scalars=0, hbm=()):
    smem = pl.BlockSpec(memory_space=pltpu.SMEM)
    vmem = pl.BlockSpec(memory_space=pltpu.VMEM)
    raw = pl.BlockSpec(memory_space=pl.ANY)
    specs = [smem if i < scalars else raw if i in hbm else vmem for i in range(len(args))]
    return pl.pallas_call(
        body,
        out_shape=outs,
        in_specs=specs,
        out_specs=jax.tree.map(lambda _: vmem, outs),
        scratch_shapes=scratch,
        compiler_params=pltpu.CompilerParams(vmem_limit_bytes=24 << 20),
        interpret=INTERPRET,
    )(*args)


def shape(dims, dtype):
    return jax.ShapeDtypeStruct(dims, dtype)


def head_columns(k):
    return slice(k * HEAD_SIZE, (k + 1) * HEAD_SIZE)


def dot_last(a, b):
    return lax.dot_general(a, b, (((1,), (1,)), ((), ())), preferred_element_type=f32)


def dot_first(a, b):
    return lax.dot_general(a, b, (((0,), (0,)), ((), ())), preferred_element_type=f32)


def prefix_body(block_ref, q_ref, k_ref, v_ref, out_ref, own_ref, q_rows, stats):
    rows = q_ref.shape[0]
    dests = out_ref.shape[0]
    per_dest = rows * GROUP // dests
    stats[...] = jnp.zeros(stats.shape, f32)
    start = pl.multiple_of(block_ref[0] * per_dest, per_dest)
    for k in range(KEY_VALUE_HEADS):
        for j in range(GROUP):
            part = q_ref[:, head_columns(k * GROUP + j)].astype(f32)
            q_rows[k, pl.ds(j, rows, stride=GROUP), :] = part
    for k in range(KEY_VALUE_HEADS):
        own_ref[k * per_dest : (k + 1) * per_dest, :] = q_rows[k, pl.ds(start, per_dest), :]
        q = q_rows[k].astype(bf16)
        scores = dot_last(k_ref[:, head_columns(k)], q) * score_scale
        top = jnp.max(scores, 0, keepdims=True)
        top_high = top.astype(bf16).astype(f32)
        top_low = (top - top_high).astype(bf16).astype(f32)
        terms = jnp.exp(scores - (top_high + top_low))
        mass = jnp.sum(terms, 0, keepdims=True)
        mass_high = mass.astype(bf16).astype(f32)
        width = rows * GROUP
        stats[k : k + 1, 0:width] = top_high
        stats[4 + k : 5 + k, 0:width] = top_low
        stats[8 + k : 9 + k, 0:width] = mass_high
        stats[12 + k : 13 + k, 0:width] = mass - mass_high
        weighted = dot_first(terms.astype(bf16), v_ref[:, head_columns(k)])
        out_ref[:, k * per_dest : (k + 1) * per_dest, :] = weighted.astype(bf16).reshape(
            dests, per_dest, HEAD_SIZE
        )
    held = stats[...]
    first = KEY_VALUE_HEADS * per_dest
    for d in range(dests):
        piece = held[:, d * per_dest : d * per_dest + LANES]
        out_ref[d, first : first + STAT_ROWS, :] = piece.astype(bf16)


def suffix_body(length_ref, own_ref, k_ref, v_ref, out_ref, stat_ref):
    per_dest = own_ref.shape[0] // KEY_VALUE_HEADS
    keys = k_ref.shape[0]
    half = keys // 2
    row = lax.broadcasted_iota(jnp.int32, (keys, per_dest), 0)
    lane = lax.broadcasted_iota(jnp.int32, (keys, per_dest), 1)
    second = row >= half
    limit = jnp.where(second, length_ref[0, 1] + half, length_ref[0, 0])
    inside = (second == (lane >= GROUP)) & (row < limit)
    stat_ref[...] = jnp.zeros(stat_ref.shape, f32)
    for k in range(KEY_VALUE_HEADS):
        q = own_ref[k * per_dest : (k + 1) * per_dest, :].astype(bf16)
        scores = dot_last(k_ref[:, head_columns(k)], q) * score_scale
        scores = jnp.where(inside, scores, masked_score)
        top = jnp.max(scores, 0, keepdims=True)
        terms = jnp.where(inside, jnp.exp(scores - top), 0.0)
        mass = jnp.sum(terms, 0, keepdims=True)
        for r in (k, 4 + k):
            stat_ref[r : r + 1, 0:per_dest] = top
            stat_ref[8 + r : 9 + r, 0:per_dest] = mass
        out_ref[k * per_dest : (k + 1) * per_dest, :] = dot_first(
            terms.astype(bf16), v_ref[:, head_columns(k)]
        )


def merge_body(part_ref, suffix_ref, stat_ref, chosen_ref, out_ref, rows):
    sources = part_ref.shape[0]
    per_dest = suffix_ref.shape[0] // KEY_VALUE_HEADS
    first = KEY_VALUE_HEADS * per_dest
    tops, masses = [stat_ref[0:8]], [stat_ref[8:16]]
    for g in range(sources):
        held = part_ref[g, first : first + STAT_ROWS, :].astype(f32)
        tops.append(held[0:8] + pltpu.roll(held[0:8], 4, 0))
        masses.append(held[8:16] + pltpu.roll(held[8:16], 4, 0))
    top = tops[0]
    for t in tops[1:]:
        top = jnp.maximum(top, t)
    scales = [jnp.exp(t - top) for t in tops]
    total = scales[0] * masses[0]
    for s, m in zip(scales[1:], masses[1:]):
        total = total + s * m
    inverse = 1.0 / total
    scales = [s * inverse for s in scales]
    scales += [jnp.zeros((8, LANES), f32)] * (-len(scales) % 16)
    table = jnp.concatenate(scales, 0)
    turned = jnp.concatenate(
        [table[i : i + LANES].T[0:per_dest] for i in range(0, table.shape[0], LANES)], 1
    )
    rows[...] = jnp.zeros(rows.shape, f32)
    for k in range(KEY_VALUE_HEADS):
        mine = slice(k * per_dest, (k + 1) * per_dest)
        mixed = turned[:, k : k + 1] * suffix_ref[mine, :]
        for g in range(sources):
            at = (g + 1) * 8 + k
            mixed = mixed + turned[:, at : at + 1] * part_ref[g, mine, :].astype(f32)
        for i in range(per_dest // GROUP):
            at = k * GROUP * DEST_ROWS + i
            rows[pl.ds(at, GROUP, stride=DEST_ROWS), :] = mixed[i * GROUP : (i + 1) * GROUP]
    for i in range(per_dest // GROUP):
        line = jnp.broadcast_to(chosen_ref[i : i + 1, :], (QUERY_HEADS, LANES))
        rows[pl.ds(2 + i, QUERY_HEADS, stride=DEST_ROWS), :] = line
    out_ref[...] = rows[...].astype(bf16)


def project_body(attn_ref, weight_ref, out_ref, chosen_ref, rows, lines):
    count = attn_ref.shape[0] // DEST_ROWS
    blocks = weight_ref.shape[1] // LANES
    rows[...] = attn_ref[...].astype(f32)
    attn = jnp.concatenate([rows[pl.ds(i, count, stride=DEST_ROWS), :] for i in range(2)], 0)
    for i in range(2):
        chosen_ref[i * count : (i + 1) * count, :] = rows[pl.ds(2 + i, count, stride=DEST_ROWS), :]
    made = jnp.dot(attn.astype(bf16), weight_ref[...], preferred_element_type=f32)
    spread_rows(made, lines, count, blocks)
    out_ref[...] = lines[...].astype(bf16)


def spread_rows(made, lines, count, blocks):
    for i in range(2):
        for c in range(blocks):
            lines[pl.ds(i * blocks + c, count, stride=2 * blocks), :] = made[
                i * count : (i + 1) * count, c * LANES : (c + 1) * LANES
            ]


def norm_body(part_ref, residual_ref, gain_ref, hidden_ref, out_ref, lines):
    sources, size, _ = part_ref.shape
    blocks = size // 2
    for c in range(blocks):
        piece = residual_ref[:, c * LANES : (c + 1) * LANES].astype(f32)
        lines[pl.ds(c, 2, stride=blocks), :] = piece
    hidden = lines[...]
    for s in range(sources):
        hidden = hidden + part_ref[s].astype(f32)
    hidden_ref[...] = hidden
    halves = []
    for i in range(2):
        half = hidden[i * blocks : (i + 1) * blocks]
        mean_square = jnp.sum(half * half, keepdims=True) / (blocks * LANES)
        halves.append(half * lax.rsqrt(mean_square + norm_epsilon) * gain_ref[...])
    normed = jnp.concatenate(halves, 0).astype(bf16)
    for s in range(sources):
        out_ref[s] = normed


def expert_body(
    first_ref, x_ref, chosen_ref, router_ref, gate_hbm, up_hbm, down_hbm, out_ref,
    lines, x_rows, gate, up, down, sems,
):
    experts = gate.shape[0]
    copies = []
    for e in range(experts):
        for n, (source, target) in enumerate(((gate_hbm, gate), (up_hbm, up), (down_hbm, down))):
            copy = pltpu.make_async_copy(source.at[e], target.at[e], sems.at[3 * e + n])
            copy.start()
            copies.append(copy)
    count, size, _ = x_ref.shape
    blocks = size // 2
    lines[...] = x_ref[...].reshape(count * size, LANES).astype(f32)
    for i in range(2):
        for c in range(blocks):
            x_rows[i * count : (i + 1) * count, c * LANES : (c + 1) * LANES] = lines[
                pl.ds(i * blocks + c, count, stride=size), :
            ].astype(bf16)
    x = x_rows[...]
    logits = jnp.dot(x, router_ref[...], preferred_element_type=f32)
    expo = jnp.where(chosen_ref[:, 0 : logits.shape[1]] > 0.5, jnp.exp(logits), 0.0)
    lane = lax.broadcasted_iota(jnp.int32, logits.shape, 1)
    mass = jnp.sum(expo, 1, keepdims=True)
    mixed = jnp.zeros((2 * count, down.shape[2]), f32)
    for e in range(experts):
        copies[3 * e].wait()
        gate_out = jnp.dot(x, gate[e], preferred_element_type=f32)
        copies[3 * e + 1].wait()
        up_out = jnp.dot(x, up[e], preferred_element_type=f32)
        act = (gate_out / (1.0 + jnp.exp(-gate_out)) * up_out).astype(bf16)
        copies[3 * e + 2].wait()
        made = jnp.dot(act, down[e], preferred_element_type=f32).astype(bf16).astype(f32)
        mine = jnp.sum(jnp.where(lane == first_ref[0] + e, expo, 0.0), 1, keepdims=True)
        mixed = mixed + (mine / mass) * made
    spread_rows(mixed, lines, count, blocks)
    out_ref[...] = lines[...].astype(bf16).reshape(count, size, LANES)


def final_body(part_ref, hidden_ref, out_ref, lines):
    sources, size, _ = part_ref.shape
    blocks = size // 2
    total = part_ref[0].astype(f32)
    for s in range(1, sources):
        total = total + part_ref[s].astype(f32)
    lines[...] = hidden_ref[...] + total
    for c in range(blocks):
        out_ref[:, c * LANES : (c + 1) * LANES] = lines[pl.ds(c, 2, stride=blocks), :]


def prefix_attention(block, q, k, v, dests):
    rows = q.shape[0]
    per_dest = rows * GROUP // dests
    send = KEY_VALUE_HEADS * per_dest + STAT_ROWS
    padded = (rows * GROUP // LANES + 1) * LANES
    return kernel_call(
        prefix_body,
        (shape((dests, send, HEAD_SIZE), bf16), shape((KEY_VALUE_HEADS * per_dest, HEAD_SIZE), f32)),
        [
            pltpu.VMEM((KEY_VALUE_HEADS, rows * GROUP, HEAD_SIZE), f32),
            pltpu.VMEM((STAT_ROWS, padded), f32),
        ],
        block, q, k, v, scalars=1,
    )


def suffix_attention(lengths, own, k, v):
    return kernel_call(
        suffix_body,
        (shape(own.shape, f32), shape((STAT_ROWS, LANES), f32)),
        [], lengths, own, k, v, scalars=1,
    )


def merge_parts(parts, suffix, stats, chosen):
    dims = (QUERY_HEADS * DEST_ROWS, HEAD_SIZE)
    return kernel_call(
        merge_body, shape(dims, bf16), [pltpu.VMEM(dims, f32)], parts, suffix, stats, chosen
    )


def project(attn, weight):
    count = attn.shape[0] // DEST_ROWS
    dims = (count * 2 * weight.shape[1] // LANES, LANES)
    return kernel_call(
        project_body,
        (shape(dims, bf16), shape((2 * count, LANES), f32)),
        [pltpu.VMEM(attn.shape, f32), pltpu.VMEM(dims, f32)],
        attn, weight,
    )


def normalize(parts, residual, gain):
    return kernel_call(
        norm_body,
        (shape(parts.shape[1:], f32), shape(parts.shape, bf16)),
        [pltpu.VMEM(parts.shape[1:], f32)],
        parts, residual, gain,
    )


def run_experts(first, x, chosen, router, gate, up, down):
    count, size, _ = x.shape
    return kernel_call(
        expert_body,
        shape(x.shape, bf16),
        [
            pltpu.VMEM((count * size, LANES), f32),
            pltpu.VMEM((2 * count, size // 2 * LANES), bf16),
            pltpu.VMEM(gate.shape, bf16),
            pltpu.VMEM(up.shape, bf16),
            pltpu.VMEM(down.shape, bf16),
            pltpu.SemaphoreType.DMA((3 * gate.shape[0],)),
        ],
        first, x, chosen, router, gate, up, down, scalars=1, hbm=(4, 5, 6),
    )


def add_parts(parts, hidden):
    size = parts.shape[1]
    return kernel_call(
        final_body,
        shape((2, size // 2 * LANES), f32),
        [pltpu.VMEM((size, LANES), f32)],
        parts, hidden,
    )


def chosen_lines(ids):
    mask = jnp.any(ids[..., None] == jnp.arange(LANES, dtype=jnp.int32), 1)
    return mask.astype(f32)


def shards(
    queries,
    shared_prefix_keys,
    shared_prefix_values,
    row_suffix_keys,
    row_suffix_values,
    suffix_lengths,
    residual,
    out_weight,
    norm_gain,
    router_weight,
    gate_weights,
    up_weights,
    down_weights,
    expert_ids,
):
    heads = lax.axis_size("head")
    dests = lax.axis_size("grp")
    block = lax.axis_index("grp").astype(jnp.int32).reshape(1)
    send, own = prefix_attention(
        block, queries[0], shared_prefix_keys[0], shared_prefix_values[0], dests
    )
    arrived = exchange(send, "grp")
    chosen = chosen_lines(expert_ids[0])
    suffix, stats = suffix_attention(
        suffix_lengths,
        own,
        row_suffix_keys.reshape(-1, row_suffix_keys.shape[-1]),
        row_suffix_values.reshape(-1, row_suffix_values.shape[-1]),
    )
    attn = merge_parts(arrived, suffix, stats, chosen)
    attn = exchange(attn.reshape(heads, DEST_ROWS, HEAD_SIZE), "head")
    parts, chosen = project(attn.reshape(heads * DEST_ROWS, HEAD_SIZE), out_weight)
    parts = exchange(parts.reshape(heads, -1, LANES), "head")
    hidden, normed = normalize(parts, residual[0], norm_gain.reshape(-1, LANES))
    x = exchange(normed, "head")
    first = (lax.axis_index("head") * gate_weights.shape[0]).astype(jnp.int32).reshape(1)
    made = run_experts(first, x, chosen, router_weight, gate_weights, up_weights, down_weights)
    return add_parts(exchange(made, "head"), hidden)[None]


def solution(mesh):
    return jax.shard_map(
        shards,
        mesh=mesh,
        in_specs=(
            P("head", None, None),
            P("head", "grp", None),
            P("head", "grp", None),
            P("head", "grp", None, None),
            P("head", "grp", None, None),
            P("head", "grp"),
            P("head", "grp", None),
            P("head", None),
            P(),
            P(),
            P("head", None, None),
            P("head", None, None),
            P("head", None, None),
            P("head", "grp", None),
        ),
        out_specs=P("head", "grp", None),
        check_vma=False,
    )
```

```python
import math

import jax
import jax.numpy as jnp
from jax import lax
from jax.experimental import pallas as pl
from jax.experimental.pallas import tpu as pltpu
from jax.sharding import PartitionSpec as P

QUERY_HEADS = 32
KEY_VALUE_HEADS = 4
HEAD_SIZE = 128
GROUP = QUERY_HEADS // KEY_VALUE_HEADS
LANES = 128
STAT_ROWS = 16
DEST_ROWS = 8

masked_score = -1e30
norm_epsilon = 1e-06
score_scale = 1.0 / math.sqrt(HEAD_SIZE)
f32 = jnp.float32
bf16 = jnp.bfloat16
INTERPRET = False


def exchange(x, axis):
    return lax.all_to_all(x, axis, split_axis=0, concat_axis=0, tiled=True)


def kernel_call(body, outs, scratch, *args, scalars=0, hbm=(), hbm_outs=()):
    smem = pl.BlockSpec(memory_space=pltpu.SMEM)
    vmem = pl.BlockSpec(memory_space=pltpu.VMEM)
    raw = pl.BlockSpec(memory_space=pltpu.HBM)
    specs = [smem if i < scalars else raw if i in hbm else vmem for i in range(len(args))]
    args = [
        pltpu.with_memory_space_constraint(a, pltpu.HBM) if i in hbm else a
        for i, a in enumerate(args)
    ]
    return pl.pallas_call(
        body,
        out_shape=outs,
        in_specs=specs,
        out_specs=tuple(raw if i in hbm_outs else vmem for i in range(len(outs))),
        scratch_shapes=scratch,
        compiler_params=pltpu.CompilerParams(vmem_limit_bytes=16 << 20),
        interpret=INTERPRET,
    )(*args)


def shape(dims, dtype):
    return jax.ShapeDtypeStruct(dims, dtype)


def head_columns(k):
    return slice(k * HEAD_SIZE, (k + 1) * HEAD_SIZE)


def dot_last(a, b):
    return lax.dot_general(a, b, (((1,), (1,)), ((), ())), preferred_element_type=f32)


def dot_first(a, b):
    return lax.dot_general(a, b, (((0,), (0,)), ((), ())), preferred_element_type=f32)


def start_copy(source, target, sem):
    copy = pltpu.make_async_copy(source, target, sem)
    copy.start()
    return copy


def prefix_body(
    block_ref, expert_ref, q_hbm, k_hbm, v_hbm, out_hbm, own_ref, mark_ref,
    q_in, k_in, v_in, q_rows, stats, made, in_sems, out_sems,
):
    rows = q_hbm.shape[0]
    dests = out_hbm.shape[0]
    per_dest = rows * GROUP // dests
    width = rows * GROUP
    wide = GROUP * HEAD_SIZE
    arrivals = []
    for k in range(KEY_VALUE_HEADS):
        q_columns = slice(k * wide, (k + 1) * wide)
        pairs = (
            (q_hbm.at[:, q_columns], q_in.at[k]),
            (k_hbm.at[:, head_columns(k)], k_in.at[k]),
            (v_hbm.at[:, head_columns(k)], v_in.at[k]),
        )
        arrivals.append([start_copy(a, b, in_sems.at[3 * k + n]) for n, (a, b) in enumerate(pairs)])
    stats[...] = jnp.zeros(stats.shape, f32)
    lane = lax.broadcasted_iota(jnp.int32, mark_ref.shape, 1)
    row = lax.broadcasted_iota(jnp.int32, mark_ref.shape, 0)
    mark_ref[...] = (lane == expert_ref[0] + row).astype(f32)
    start = pl.multiple_of(block_ref[0] * per_dest, per_dest)
    departures = []
    for k in range(KEY_VALUE_HEADS):
        for copy in arrivals[k]:
            copy.wait()
        for j in range(GROUP):
            q_rows[k, pl.ds(j, rows, stride=GROUP), :] = q_in[k, :, head_columns(j)].astype(f32)
        mine = slice(k * per_dest, (k + 1) * per_dest)
        own_ref[mine, :] = q_rows[k, pl.ds(start, per_dest), :]
        scores = dot_last(k_in[k], q_rows[k].astype(bf16)) * score_scale
        top = jnp.max(scores, 0, keepdims=True)
        top_high = top.astype(bf16).astype(f32)
        top_low = (top - top_high).astype(bf16).astype(f32)
        terms = jnp.exp(scores - (top_high + top_low))
        mass = jnp.sum(terms, 0, keepdims=True)
        mass_high = mass.astype(bf16).astype(f32)
        stats[k : k + 1, 0:width] = top_high
        stats[4 + k : 5 + k, 0:width] = top_low
        stats[8 + k : 9 + k, 0:width] = mass_high
        stats[12 + k : 13 + k, 0:width] = mass - mass_high
        weighted = dot_first(terms.astype(bf16), v_in[k])
        made[:, mine, :] = weighted.astype(bf16).reshape(dests, per_dest, HEAD_SIZE)
        departures.append(start_copy(made.at[:, mine, :], out_hbm.at[:, mine, :], out_sems.at[k]))
    held = stats[...]
    last = slice(KEY_VALUE_HEADS * per_dest, KEY_VALUE_HEADS * per_dest + STAT_ROWS)
    for d in range(dests):
        made[d, last, :] = held[:, d * per_dest : d * per_dest + LANES].astype(bf16)
    departures.append(
        start_copy(made.at[:, last, :], out_hbm.at[:, last, :], out_sems.at[KEY_VALUE_HEADS])
    )
    for copy in departures:
        copy.wait()


def window_body(
    length_ref, own_ref, k_hbm, v_hbm, residual_hbm, gain_hbm, out_ref, stat_ref, lines_ref,
    gain_ref, k_ref, v_ref, residual_ref, sems,
):
    pairs = (
        (k_hbm, k_ref),
        (v_hbm, v_ref),
        (residual_hbm, residual_ref),
        (gain_hbm, gain_ref),
    )
    copies = [start_copy(a, b, sems.at[n]) for n, (a, b) in enumerate(pairs)]
    for copy in copies:
        copy.wait()
    blocks = lines_ref.shape[0] // 2
    for c in range(blocks):
        piece = residual_ref[:, c * LANES : (c + 1) * LANES].astype(f32)
        lines_ref[pl.ds(c, 2, stride=blocks), :] = piece
    suffix_attention(length_ref, own_ref, k_ref, v_ref, out_ref, stat_ref)


def suffix_attention(length_ref, own_ref, k_ref, v_ref, out_ref, stat_ref):
    per_dest = own_ref.shape[0] // KEY_VALUE_HEADS
    keys = k_ref.shape[0]
    half = keys // 2
    row = lax.broadcasted_iota(jnp.int32, (keys, per_dest), 0)
    lane = lax.broadcasted_iota(jnp.int32, (keys, per_dest), 1)
    second = row >= half
    limit = jnp.where(second, length_ref[0, 1] + half, length_ref[0, 0])
    inside = (second == (lane >= GROUP)) & (row < limit)
    stat_ref[...] = jnp.zeros(stat_ref.shape, f32)
    for k in range(KEY_VALUE_HEADS):
        q = own_ref[k * per_dest : (k + 1) * per_dest, :].astype(bf16)
        scores = dot_last(k_ref[:, head_columns(k)], q) * score_scale
        scores = jnp.where(inside, scores, masked_score)
        top = jnp.max(scores, 0, keepdims=True)
        terms = jnp.where(inside, jnp.exp(scores - top), 0.0)
        mass = jnp.sum(terms, 0, keepdims=True)
        for r in (k, 4 + k):
            stat_ref[r : r + 1, 0:per_dest] = top
            stat_ref[8 + r : 9 + r, 0:per_dest] = mass
        out_ref[k * per_dest : (k + 1) * per_dest, :] = dot_first(
            terms.astype(bf16), v_ref[:, head_columns(k)]
        )


def merge_body(
    part_ref, suffix_ref, stat_ref, chosen_ref, weight_hbm, router_hbm, up_hbm,
    out_ref, weight_ref, router_ref, up_ref, rows, sems,
):
    pairs = ((weight_hbm, weight_ref), (router_hbm, router_ref), (up_hbm, up_ref))
    copies = [start_copy(a, b, sems.at[n]) for n, (a, b) in enumerate(pairs)]
    sources = part_ref.shape[0]
    per_dest = suffix_ref.shape[0] // KEY_VALUE_HEADS
    first = KEY_VALUE_HEADS * per_dest
    tops, masses = [stat_ref[0:8]], [stat_ref[8:16]]
    for g in range(sources):
        held = part_ref[g, first : first + STAT_ROWS, :].astype(f32)
        tops.append(held[0:8] + pltpu.roll(held[0:8], 4, 0))
        masses.append(held[8:16] + pltpu.roll(held[8:16], 4, 0))
    top = tops[0]
    for t in tops[1:]:
        top = jnp.maximum(top, t)
    scales = [jnp.exp(t - top) for t in tops]
    total = scales[0] * masses[0]
    for s, m in zip(scales[1:], masses[1:]):
        total = total + s * m
    inverse = 1.0 / total
    scales = [s * inverse for s in scales]
    scales += [jnp.zeros((8, LANES), f32)] * (-len(scales) % 16)
    table = jnp.concatenate(scales, 0)
    turned = jnp.concatenate(
        [table[i : i + LANES].T[0:per_dest] for i in range(0, table.shape[0], LANES)], 1
    )
    rows[...] = jnp.zeros(rows.shape, f32)
    for k in range(KEY_VALUE_HEADS):
        mine = slice(k * per_dest, (k + 1) * per_dest)
        mixed = turned[:, k : k + 1] * suffix_ref[mine, :]
        for g in range(sources):
            at = (g + 1) * 8 + k
            mixed = mixed + turned[:, at : at + 1] * part_ref[g, mine, :].astype(f32)
        for i in range(per_dest // GROUP):
            at = k * GROUP * DEST_ROWS + i
            rows[pl.ds(at, GROUP, stride=DEST_ROWS), :] = mixed[i * GROUP : (i + 1) * GROUP]
    for i in range(per_dest // GROUP):
        line = jnp.broadcast_to(chosen_ref[i : i + 1, :], (QUERY_HEADS, LANES))
        rows[pl.ds(2 + i, QUERY_HEADS, stride=DEST_ROWS), :] = line
    out_ref[...] = rows[...].astype(bf16)
    for copy in copies:
        copy.wait()


def project_body(attn_ref, weight_ref, out_ref, chosen_ref, rows, lines):
    count = attn_ref.shape[0] // DEST_ROWS
    blocks = weight_ref.shape[1] // LANES
    rows[...] = attn_ref[...].astype(f32)
    attn = jnp.concatenate([rows[pl.ds(i, count, stride=DEST_ROWS), :] for i in range(2)], 0)
    for i in range(2):
        chosen_ref[i * count : (i + 1) * count, :] = rows[pl.ds(2 + i, count, stride=DEST_ROWS), :]
    made = jnp.dot(attn.astype(bf16), weight_ref[...], preferred_element_type=f32)
    spread_rows(made, lines, count, blocks)
    out_ref[...] = lines[...].astype(bf16)


def spread_rows(made, lines, count, blocks):
    for i in range(2):
        for c in range(blocks):
            lines[pl.ds(i * blocks + c, count, stride=2 * blocks), :] = made[
                i * count : (i + 1) * count, c * LANES : (c + 1) * LANES
            ]


def norm_body(part_ref, residual_ref, gain_ref, hidden_ref, out_ref):
    sources, size, _ = part_ref.shape
    blocks = size // 2
    hidden = residual_ref[...]
    for s in range(sources):
        hidden = hidden + part_ref[s].astype(f32)
    hidden_ref[...] = hidden
    halves = []
    for i in range(2):
        half = hidden[i * blocks : (i + 1) * blocks]
        mean_square = jnp.sum(half * half, keepdims=True) / (blocks * LANES)
        halves.append(half * lax.rsqrt(mean_square + norm_epsilon) * gain_ref[...])
    normed = jnp.concatenate(halves, 0).astype(bf16)
    for s in range(sources):
        out_ref[s] = normed


def expert_body(
    x_ref, chosen_ref, mark_ref, router_ref, gate, up, down_hbm, out_ref,
    lines, x_rows, down, sems,
):
    experts = gate.shape[0]
    copies = [start_copy(down_hbm.at[e], down.at[e], sems.at[e]) for e in range(experts)]
    count, size, _ = x_ref.shape
    blocks = size // 2
    lines[...] = x_ref[...].reshape(count * size, LANES).astype(f32)
    for i in range(2):
        for c in range(blocks):
            x_rows[i * count : (i + 1) * count, c * LANES : (c + 1) * LANES] = lines[
                pl.ds(i * blocks + c, count, stride=size), :
            ].astype(bf16)
    x = x_rows[...]
    logits = dot_last(x, router_ref[...])
    expo = jnp.where(chosen_ref[:, 0 : logits.shape[1]] > 0.5, jnp.exp(logits), 0.0)
    mass = jnp.sum(expo, 1, keepdims=True)
    mixed = jnp.zeros((2 * count, down.shape[2]), f32)
    for e in range(experts):
        gate_out = jnp.dot(x, gate[e], preferred_element_type=f32)
        up_out = jnp.dot(x, up[e], preferred_element_type=f32)
        act = (gate_out / (1.0 + jnp.exp(-gate_out)) * up_out).astype(bf16)
        copies[e].wait()
        made = jnp.dot(act, down[e], preferred_element_type=f32).astype(bf16).astype(f32)
        mark = mark_ref[e : e + 1, 0 : expo.shape[1]] > 0.5
        mine = jnp.sum(jnp.where(mark, expo, 0.0), 1, keepdims=True)
        mixed = mixed + (mine / mass) * made
    spread_rows(mixed, lines, count, blocks)
    out_ref[...] = lines[...].astype(bf16).reshape(count, size, LANES)


def final_body(part_ref, hidden_ref, out_ref, lines):
    sources, size, _ = part_ref.shape
    blocks = size // 2
    total = part_ref[0].astype(f32)
    for s in range(1, sources):
        total = total + part_ref[s].astype(f32)
    lines[...] = hidden_ref[...] + total
    for c in range(blocks):
        out_ref[:, c * LANES : (c + 1) * LANES] = lines[pl.ds(c, 2, stride=blocks), :]


def prefix_attention(block, expert, q, k, v, dests):
    rows = q.shape[0]
    per_dest = rows * GROUP // dests
    send = (dests, KEY_VALUE_HEADS * per_dest + STAT_ROWS, HEAD_SIZE)
    padded = (rows * GROUP // LANES + 1) * LANES
    made, own, marks = kernel_call(
        prefix_body,
        (
            pltpu.HBM(send, bf16),
            shape((KEY_VALUE_HEADS * per_dest, HEAD_SIZE), f32),
            shape((8, LANES), f32),
        ),
        [
            pltpu.VMEM((KEY_VALUE_HEADS, rows, GROUP * HEAD_SIZE), bf16),
            pltpu.VMEM((KEY_VALUE_HEADS, k.shape[0], HEAD_SIZE), bf16),
            pltpu.VMEM((KEY_VALUE_HEADS, k.shape[0], HEAD_SIZE), bf16),
            pltpu.VMEM((KEY_VALUE_HEADS, rows * GROUP, HEAD_SIZE), f32),
            pltpu.VMEM((STAT_ROWS, padded), f32),
            pltpu.VMEM(send, bf16),
            pltpu.SemaphoreType.DMA((3 * KEY_VALUE_HEADS,)),
            pltpu.SemaphoreType.DMA((KEY_VALUE_HEADS + 1,)),
        ],
        block, expert, q, k, v, scalars=2, hbm=(2, 3, 4), hbm_outs=(0,),
    )
    return made, own, marks


def fill_window(lengths, own, k, v, residual, gain):
    return kernel_call(
        window_body,
        (
            shape(own.shape, f32),
            shape((STAT_ROWS, LANES), f32),
            shape((residual.size // LANES, LANES), f32),
            shape(gain.shape, f32),
        ),
        [pltpu.VMEM(a.shape, bf16) for a in (k, v, residual)]
        + [pltpu.SemaphoreType.DMA((4,))],
        lengths, own, k, v, residual, gain, scalars=1, hbm=(2, 3, 4, 5),
    )


def merge_parts(parts, suffix, stats, chosen, *weights):
    dims = (QUERY_HEADS * DEST_ROWS, HEAD_SIZE)
    return kernel_call(
        merge_body,
        (shape(dims, bf16), *(shape(w.shape, bf16) for w in weights)),
        [pltpu.VMEM(dims, f32), pltpu.SemaphoreType.DMA((len(weights),))],
        parts, suffix, stats, chosen, *weights, hbm=range(4, 4 + len(weights)),
    )


def project(attn, weight):
    count = attn.shape[0] // DEST_ROWS
    dims = (count * 2 * weight.shape[1] // LANES, LANES)
    return kernel_call(
        project_body,
        (shape(dims, bf16), shape((2 * count, LANES), f32)),
        [pltpu.VMEM(attn.shape, f32), pltpu.VMEM(dims, f32)],
        attn, weight,
    )


def normalize(parts, residual, gain):
    return kernel_call(
        norm_body,
        (shape(parts.shape[1:], f32), shape(parts.shape, bf16)),
        [],
        parts, residual, gain,
    )


def run_experts(x, chosen, marks, router, gate, up, down):
    count, size, _ = x.shape
    return kernel_call(
        expert_body,
        (shape(x.shape, bf16),),
        [
            pltpu.VMEM((count * size, LANES), f32),
            pltpu.VMEM((2 * count, size // 2 * LANES), bf16),
            pltpu.VMEM(down.shape, bf16),
            pltpu.SemaphoreType.DMA((down.shape[0],)),
        ],
        x, chosen, marks, router, gate, up, down, hbm=(6,),
    )[0]


def add_parts(parts, hidden):
    size = parts.shape[1]
    return kernel_call(
        final_body,
        (shape((2, size // 2 * LANES), f32),),
        [pltpu.VMEM((size, LANES), f32)],
        parts, hidden,
    )[0]


def chosen_lines(ids):
    mask = jnp.any(ids[..., None] == jnp.arange(LANES, dtype=jnp.int32), 1)
    return mask.astype(f32)


def shards(
    queries,
    shared_prefix_keys,
    shared_prefix_values,
    row_suffix_keys,
    row_suffix_values,
    suffix_lengths,
    residual,
    out_weight,
    norm_gain,
    router_weight,
    gate_weights,
    up_weights,
    down_weights,
    expert_ids,
):
    heads = lax.axis_size("head")
    dests = lax.axis_size("grp")
    block = lax.axis_index("grp").astype(jnp.int32).reshape(1)
    expert = (lax.axis_index("head") * gate_weights.shape[0]).astype(jnp.int32).reshape(1)
    send, own, marks = prefix_attention(
        block, expert, queries[0], shared_prefix_keys[0], shared_prefix_values[0], dests
    )
    arrived = exchange(send, "grp")
    chosen = chosen_lines(expert_ids[0])
    suffix, stats, residual_lines, gain = fill_window(
        suffix_lengths,
        own,
        row_suffix_keys.reshape(-1, row_suffix_keys.shape[-1]),
        row_suffix_values.reshape(-1, row_suffix_values.shape[-1]),
        residual[0],
        norm_gain.reshape(-1, LANES),
    )
    attn, weight, router, up = merge_parts(
        arrived, suffix, stats, chosen, out_weight, router_weight.T, up_weights
    )
    attn = exchange(attn.reshape(heads, DEST_ROWS, HEAD_SIZE), "head")
    parts, chosen = project(attn.reshape(heads * DEST_ROWS, HEAD_SIZE), weight)
    parts = exchange(parts.reshape(heads, -1, LANES), "head")
    hidden, normed = normalize(parts, residual_lines, gain)
    x = exchange(normed, "head")
    made = run_experts(x, chosen, marks, router, gate_weights, up, down_weights)
    return add_parts(exchange(made, "head"), hidden)[None]


def solution(mesh):
    return jax.shard_map(
        shards,
        mesh=mesh,
        in_specs=(
            P("head", None, None),
            P("head", "grp", None),
            P("head", "grp", None),
            P("head", "grp", None, None),
            P("head", "grp", None, None),
            P("head", "grp"),
            P("head", "grp", None),
            P("head", None),
            P(),
            P(),
            P("head", None, None),
            P("head", None, None),
            P("head", None, None),
            P("head", "grp", None),
        ),
        out_specs=P("head", "grp", None),
        check_vma=False,
    )
```

```python
import math

import jax
import jax.numpy as jnp
from jax import lax
from jax.experimental import pallas as pl
from jax.experimental.pallas import tpu as pltpu
from jax.sharding import PartitionSpec as P


QUERY_HEADS = 32
KEY_VALUE_HEADS = 4
HEAD_SIZE = 128
GROUP = QUERY_HEADS // KEY_VALUE_HEADS
LANES = 128
STAT_ROWS = 8
DEST_ROWS = 16
SPREAD = 4
EXTRA_ROWS = 8

masked_score = -1e30
norm_epsilon = 1e-06
score_scale = 1.0 / math.sqrt(HEAD_SIZE)
f32 = jnp.float32
bf16 = jnp.bfloat16
INTERPRET = False


def exchange(x, axis, groups=None):
    return lax.all_to_all(
        x, axis, split_axis=0, concat_axis=0, tiled=True, axis_index_groups=groups
    )


def kernel_call(body, outs, scratch, *args, scalars=0, hbm=(), hbm_outs=()):
    smem = pl.BlockSpec(memory_space=pltpu.SMEM)
    vmem = pl.BlockSpec(memory_space=pltpu.VMEM)
    raw = pl.BlockSpec(memory_space=pltpu.HBM)
    specs = [smem if i < scalars else raw if i in hbm else vmem for i in range(len(args))]
    args = [
        pltpu.with_memory_space_constraint(a, pltpu.HBM) if i in hbm else a
        for i, a in enumerate(args)
    ]
    return pl.pallas_call(
        body,
        out_shape=outs,
        in_specs=specs,
        out_specs=tuple(raw if i in hbm_outs else vmem for i in range(len(outs))),
        scratch_shapes=scratch,
        compiler_params=pltpu.CompilerParams(vmem_limit_bytes=16 << 20),
        interpret=INTERPRET,
    )(*args)


def shape(dims, dtype):
    return jax.ShapeDtypeStruct(dims, dtype)


def head_columns(k):
    return slice(k * HEAD_SIZE, (k + 1) * HEAD_SIZE)


def dot_last(a, b):
    return lax.dot_general(a, b, (((1,), (1,)), ((), ())), preferred_element_type=f32)


def dot_first(a, b):
    return lax.dot_general(a, b, (((0,), (0,)), ((), ())), preferred_element_type=f32)


def start_copy(source, target, sem):
    copy = pltpu.make_async_copy(source, target, sem)
    copy.start()
    return copy


def prefix_body(
    block_ref, expert_ref, q_hbm, k_hbm, v_hbm, out_hbm, own_ref, mark_ref,
    q_in, k_in, v_in, q_rows, stats, rests, made, in_sems, out_sems,
):
    rows = q_hbm.shape[0]
    dests = out_hbm.shape[0]
    per_dest = rows * GROUP // dests
    width = rows * GROUP
    wide = GROUP * HEAD_SIZE
    keys = start_copy(k_hbm, k_in, in_sems.at[KEY_VALUE_HEADS])
    arrivals = [
        start_copy(q_hbm.at[:, k * wide : (k + 1) * wide], q_in.at[k], in_sems.at[k])
        for k in range(KEY_VALUE_HEADS)
    ]
    values = start_copy(v_hbm, v_in, in_sems.at[KEY_VALUE_HEADS + 1])
    stats[...] = jnp.zeros(stats.shape, f32)
    rests[...] = jnp.zeros(rests.shape, f32)
    lane = lax.broadcasted_iota(jnp.int32, mark_ref.shape, 1)
    row = lax.broadcasted_iota(jnp.int32, mark_ref.shape, 0)
    mark_ref[...] = (lane == expert_ref[0] + row).astype(f32)
    start = pl.multiple_of(block_ref[0] * per_dest, per_dest)
    departures = []
    for k in range(KEY_VALUE_HEADS):
        arrivals[k].wait()
        if k == 0:
            keys.wait()
        for j in range(GROUP):
            q_rows[k, pl.ds(j, rows, stride=GROUP), :] = q_in[k, :, head_columns(j)].astype(f32)
        mine = slice(k * per_dest, (k + 1) * per_dest)
        own_ref[mine, :] = q_rows[k, pl.ds(start, per_dest), :]
        scores = dot_last(k_in[:, head_columns(k)], q_rows[k].astype(bf16)) * score_scale
        top = jnp.max(scores, 0, keepdims=True)
        top_high = top.astype(bf16).astype(f32)
        top_low = (top - top_high).astype(bf16).astype(f32)
        terms = jnp.exp(scores - (top_high + top_low))
        mass = jnp.sum(terms, 0, keepdims=True)
        mass_high = mass.astype(bf16).astype(f32)
        stats[k : k + 1, 0:width] = top_high
        stats[4 + k : 5 + k, 0:width] = mass_high
        rests[k : k + 1, 0:width] = top_low
        rests[4 + k : 5 + k, 0:width] = mass - mass_high
        if k == 0:
            values.wait()
        weighted = dot_first(terms.astype(bf16), v_in[:, head_columns(k)])
        made[:, mine, :] = weighted.astype(bf16).reshape(dests, per_dest, HEAD_SIZE)
        departures.append(start_copy(made.at[:, mine, :], out_hbm.at[:, mine, :], out_sems.at[k]))
    held = stats[...]
    rest = pltpu.roll(rests[...], per_dest, 1)
    low = lax.broadcasted_iota(jnp.int32, (STAT_ROWS, LANES), 1) < per_dest
    last = slice(KEY_VALUE_HEADS * per_dest, KEY_VALUE_HEADS * per_dest + STAT_ROWS)
    for d in range(dests):
        at = slice(d * per_dest, d * per_dest + LANES)
        made[d, last, :] = jnp.where(low, held[:, at], rest[:, at]).astype(bf16)
    departures.append(
        start_copy(made.at[:, last, :], out_hbm.at[:, last, :], out_sems.at[KEY_VALUE_HEADS])
    )
    for copy in departures:
        copy.wait()


def pack_body(place_ref, weight_hbm, residual_hbm, *refs):
    outs, (weight, residual, extra, extras, sems) = refs[:SPREAD], refs[SPREAD:]
    depth, width = weight.shape[0], outs[0].shape[1]
    load = start_copy(weight_hbm, weight, sems.at[0])
    small = start_copy(residual_hbm, residual, sems.at[1])
    small.wait()
    copies = []
    starts = []
    for s in range(SPREAD):
        start = pl.multiple_of(((place_ref[0] + s) & (SPREAD - 1)) * width, width)
        starts.append(start)
        extra[...] = jnp.zeros(extra.shape, f32)
        extra[0:2, :] = residual[:, pl.ds(start, width)].astype(f32)
        extras[s] = extra[...].astype(bf16)
        copies.append(
            start_copy(extras.at[s], outs[s].at[depth : depth + EXTRA_ROWS, :], sems.at[2 + s])
        )
    load.wait()
    for s in range(SPREAD):
        piece = weight.at[:, pl.ds(starts[s], width)]
        copies.append(start_copy(piece, outs[s].at[0:depth, :], sems.at[2 + SPREAD + s]))
    for copy in copies:
        copy.wait()


def window_body(length_ref, own_ref, k_hbm, v_hbm, out_ref, stat_ref, k_ref, v_ref, sems):
    pairs = ((k_hbm, k_ref), (v_hbm, v_ref))
    copies = [start_copy(a, b, sems.at[n]) for n, (a, b) in enumerate(pairs)]
    for copy in copies:
        copy.wait()
    suffix_attention(length_ref, own_ref, k_ref, v_ref, out_ref, stat_ref)


def suffix_attention(length_ref, own_ref, k_ref, v_ref, out_ref, stat_ref):
    per_dest = own_ref.shape[0] // KEY_VALUE_HEADS
    keys = k_ref.shape[0]
    half = keys // 2
    row = lax.broadcasted_iota(jnp.int32, (keys, per_dest), 0)
    lane = lax.broadcasted_iota(jnp.int32, (keys, per_dest), 1)
    second = row >= half
    limit = jnp.where(second, length_ref[0, 1] + half, length_ref[0, 0])
    inside = (second == (lane >= GROUP)) & (row < limit)
    stat_ref[...] = jnp.zeros(stat_ref.shape, f32)
    for k in range(KEY_VALUE_HEADS):
        q = own_ref[k * per_dest : (k + 1) * per_dest, :].astype(bf16)
        scores = dot_last(k_ref[:, head_columns(k)], q) * score_scale
        scores = jnp.where(inside, scores, masked_score)
        top = jnp.max(scores, 0, keepdims=True)
        terms = jnp.where(inside, jnp.exp(scores - top), 0.0)
        mass = jnp.sum(terms, 0, keepdims=True)
        stat_ref[k : k + 1, 0:per_dest] = top
        stat_ref[4 + k : 5 + k, 0:per_dest] = mass
        out_ref[k * per_dest : (k + 1) * per_dest, :] = dot_first(
            terms.astype(bf16), v_ref[:, head_columns(k)]
        )


def merge_body(
    part_ref, suffix_ref, stat_ref, chosen_ref, router_hbm, up_hbm,
    out_ref, router_ref, up_ref, rows, heads, sems,
):
    pairs = ((router_hbm, router_ref), (up_hbm, up_ref))
    copies = [start_copy(a, b, sems.at[n]) for n, (a, b) in enumerate(pairs)]
    sources = part_ref.shape[0]
    per_dest = suffix_ref.shape[0] // KEY_VALUE_HEADS
    first = KEY_VALUE_HEADS * per_dest
    held = [stat_ref[...]]
    for g in range(sources):
        both = part_ref[g, first : first + STAT_ROWS, :].astype(f32)
        held.append(both + pltpu.roll(both, LANES - per_dest, 1))
    top = held[0]
    for t in held[1:]:
        top = jnp.maximum(top, t)
    scales = [jnp.exp(t - top) for t in held]
    masses = [pltpu.roll(t, 4, 0) for t in held]
    total = scales[0] * masses[0]
    for s, m in zip(scales[1:], masses[1:]):
        total = total + s * m
    inverse = 1.0 / total
    scales = [s * inverse for s in scales]
    scales += [jnp.zeros((8, LANES), f32)] * (-len(scales) % 16)
    table = jnp.concatenate(scales, 0)
    turned = jnp.concatenate(
        [table[i : i + LANES].T[0:per_dest] for i in range(0, table.shape[0], LANES)], 1
    )
    rows[...] = jnp.zeros(rows.shape, f32)
    for k in range(KEY_VALUE_HEADS):
        mine = slice(k * per_dest, (k + 1) * per_dest)
        mixed = turned[:, k : k + 1] * suffix_ref[mine, :]
        for g in range(sources):
            at = (g + 1) * 8 + k
            mixed = mixed + turned[:, at : at + 1] * part_ref[g, mine, :].astype(f32)
        for i in range(2):
            heads[i * QUERY_HEADS + k * GROUP : i * QUERY_HEADS + (k + 1) * GROUP, :] = mixed[
                i * GROUP : (i + 1) * GROUP
            ]
    near = QUERY_HEADS // SPREAD
    for y in range(SPREAD):
        for s in range(SPREAD):
            source = (y - s) % SPREAD * near
            for i in range(2):
                at = y * near * DEST_ROWS + i * SPREAD + s
                rows[pl.ds(at, near, stride=DEST_ROWS), :] = heads[
                    i * QUERY_HEADS + source : i * QUERY_HEADS + source + near, :
                ]
    for i in range(2):
        line = jnp.broadcast_to(chosen_ref[i : i + 1, :], (QUERY_HEADS, LANES))
        rows[pl.ds(2 * SPREAD + i, QUERY_HEADS, stride=DEST_ROWS), :] = line
    out_ref[...] = rows[...].astype(bf16)
    for copy in copies:
        copy.wait()


def project_body(place_ref, attn_ref, *refs):
    pieces, (out_ref, chosen_ref, residual_ref, rows, lines) = refs[:SPREAD], refs[SPREAD:]
    count = attn_ref.shape[0] // DEST_ROWS
    depth = pieces[0].shape[0] - EXTRA_ROWS
    near = count // SPREAD
    blocks = pieces[0].shape[1] // LANES
    rows[...] = attn_ref[...].astype(f32)
    for i in range(2):
        line = rows[pl.ds(2 * SPREAD + i, count, stride=DEST_ROWS), :]
        chosen_ref[i * count : (i + 1) * count, :] = line
    made = jnp.zeros((2 * count, blocks * LANES), f32)
    for s in range(SPREAD):
        attn = [rows[pl.ds(i * SPREAD + s, count, stride=DEST_ROWS), :] for i in range(2)]
        attn = jnp.concatenate(attn, 0).astype(bf16)
        made = made + jnp.dot(attn, pieces[s][0:depth, :], preferred_element_type=f32)
        extra = pieces[s][depth : depth + EXTRA_ROWS, :].astype(f32)
        source = (place_ref[0] + SPREAD - s) & (SPREAD - 1)
        for i in range(2):
            for c in range(blocks):
                residual_ref[pl.ds(c * 2 * SPREAD + i * SPREAD + source, 1), :] = extra[
                    i : i + 1, c * LANES : (c + 1) * LANES
                ]
    for c in range(blocks):
        lines[c] = made[:, c * LANES : (c + 1) * LANES]
    for n in range(near):
        parts = [lines[c, pl.ds(n, 2 * SPREAD, stride=near), :] for c in range(blocks)]
        out_ref[n] = jnp.concatenate(parts, 0).astype(bf16)


def spread_rows(made, lines, count, blocks):
    for i in range(2):
        for c in range(blocks):
            lines[pl.ds(i * blocks + c, count, stride=2 * blocks), :] = made[
                i * count : (i + 1) * count, c * LANES : (c + 1) * LANES
            ]


def sum_body(part_ref, residual_ref, out_ref):
    hidden = residual_ref[...]
    for n in range(part_ref.shape[0]):
        hidden = hidden + part_ref[n].astype(f32)
    hidden = hidden.astype(bf16)
    for h in range(out_ref.shape[0]):
        out_ref[h] = hidden


def expert_body(
    first_ref, x_ref, chosen_ref, mark_ref, gain_ref, router_ref, gate, up, down_hbm,
    out_ref, hidden_ref, lines, x_rows, down, sems,
):
    experts = gate.shape[0]
    copies = [start_copy(down_hbm.at[e], down.at[e], sems.at[e]) for e in range(experts)]
    count, size, _ = x_ref.shape
    near = count // SPREAD
    pairs = 2 * SPREAD
    blocks = size // pairs
    own = first_ref[0] // experts
    far = own // near
    lines[...] = x_ref[...].astype(f32).reshape(lines.shape)
    for y in range(SPREAD):
        for c in range(blocks):
            for n in range(near):
                at = (y * near + n) * size + c * pairs
                x_rows[y * blocks + c, pl.ds(n, pairs, stride=near), :] = lines[at : at + pairs, :]
            for i in range(2):
                at = (y * near + own - far * near) * size + c * pairs + i * SPREAD + far
                to = (i * SPREAD + y) * blocks + c
                hidden_ref[to : to + 1, :] = lines[pl.ds(at, 1), :]
    hidden = jnp.concatenate([x_rows[c] for c in range(SPREAD * blocks)], 1)
    mean_square = jnp.sum(hidden * hidden, 1, keepdims=True) / hidden.shape[1]
    x = (hidden * lax.rsqrt(mean_square + norm_epsilon) * gain_ref[...]).astype(bf16)
    logits = dot_last(x, router_ref[...])
    expo = jnp.where(chosen_ref[:, 0 : logits.shape[1]] > 0.5, jnp.exp(logits), 0.0)
    mass = jnp.sum(expo, 1, keepdims=True)
    mixed = jnp.zeros((2 * count, down.shape[2]), f32)
    for e in range(experts):
        gate_out = jnp.dot(x, gate[e], preferred_element_type=f32)
        up_out = jnp.dot(x, up[e], preferred_element_type=f32)
        act = (gate_out / (1.0 + jnp.exp(-gate_out)) * up_out).astype(bf16)
        copies[e].wait()
        made = jnp.dot(act, down[e], preferred_element_type=f32).astype(bf16).astype(f32)
        mark = mark_ref[e : e + 1, 0 : expo.shape[1]] > 0.5
        mine = jnp.sum(jnp.where(mark, expo, 0.0), 1, keepdims=True)
        mixed = mixed + (mine / mass) * made
    spread_rows(mixed, lines, count, size // 2)
    out_ref[...] = lines[...].astype(bf16).reshape(count, size, LANES)


def final_body(part_ref, hidden_ref, out_ref, lines):
    sources, size, _ = part_ref.shape
    blocks = size // 2
    total = part_ref[0].astype(f32)
    for s in range(1, sources):
        total = total + part_ref[s].astype(f32)
    lines[...] = hidden_ref[...] + total
    for c in range(blocks):
        out_ref[:, c * LANES : (c + 1) * LANES] = lines[pl.ds(c, 2, stride=blocks), :]


def prefix_attention(block, expert, q, k, v, dests):
    rows = q.shape[0]
    per_dest = rows * GROUP // dests
    send = (dests, KEY_VALUE_HEADS * per_dest + STAT_ROWS, HEAD_SIZE)
    padded = (rows * GROUP // LANES + 1) * LANES
    made, own, marks = kernel_call(
        prefix_body,
        (
            pltpu.HBM(send, bf16),
            shape((KEY_VALUE_HEADS * per_dest, HEAD_SIZE), f32),
            shape((8, LANES), f32),
        ),
        [
            pltpu.VMEM((KEY_VALUE_HEADS, rows, GROUP * HEAD_SIZE), bf16),
            pltpu.VMEM(k.shape, bf16),
            pltpu.VMEM(v.shape, bf16),
            pltpu.VMEM((KEY_VALUE_HEADS, rows * GROUP, HEAD_SIZE), f32),
            pltpu.VMEM((STAT_ROWS, padded), f32),
            pltpu.VMEM((STAT_ROWS, padded), f32),
            pltpu.VMEM(send, bf16),
            pltpu.SemaphoreType.DMA((KEY_VALUE_HEADS + 2,)),
            pltpu.SemaphoreType.DMA((KEY_VALUE_HEADS + 1,)),
        ],
        block, expert, q, k, v, scalars=2, hbm=(2, 3, 4), hbm_outs=(0,),
    )
    return made, own, marks


def pack_weights(place, weight, residual):
    width = weight.shape[1] // SPREAD
    dims = (weight.shape[0] + EXTRA_ROWS, width)
    return kernel_call(
        pack_body,
        tuple(pltpu.HBM(dims, bf16) for _ in range(SPREAD)),
        [
            pltpu.VMEM(weight.shape, bf16),
            pltpu.VMEM(residual.shape, bf16),
            pltpu.VMEM((EXTRA_ROWS, width), f32),
            pltpu.VMEM((SPREAD, EXTRA_ROWS, width), bf16),
            pltpu.SemaphoreType.DMA((2 + 2 * SPREAD,)),
        ],
        place, weight, residual, scalars=1, hbm=(1, 2), hbm_outs=range(SPREAD),
    )


def fill_window(lengths, own, k, v):
    return kernel_call(
        window_body,
        (shape(own.shape, f32), shape((STAT_ROWS, LANES), f32)),
        [pltpu.VMEM(k.shape, bf16), pltpu.VMEM(v.shape, bf16), pltpu.SemaphoreType.DMA((2,))],
        lengths, own, k, v, scalars=1, hbm=(2, 3),
    )


def merge_parts(parts, suffix, stats, chosen, *weights):
    dims = (QUERY_HEADS * DEST_ROWS, HEAD_SIZE)
    return kernel_call(
        merge_body,
        (shape(dims, bf16), *(shape(w.shape, bf16) for w in weights)),
        [
            pltpu.VMEM(dims, f32),
            pltpu.VMEM((2 * QUERY_HEADS, HEAD_SIZE), f32),
            pltpu.SemaphoreType.DMA((len(weights),)),
        ],
        parts, suffix, stats, chosen, *weights, hbm=range(4, 4 + len(weights)),
    )


def project(place, attn, pieces):
    count = attn.shape[0] // DEST_ROWS
    near, blocks = count // SPREAD, pieces[0].shape[1] // LANES
    size = 2 * SPREAD * blocks
    return kernel_call(
        project_body,
        (
            shape((near, size, LANES), bf16),
            shape((2 * count, LANES), f32),
            shape((size, LANES), f32),
        ),
        [pltpu.VMEM(attn.shape, f32), pltpu.VMEM((blocks, 2 * count, LANES), f32)],
        place, attn, *pieces, scalars=1,
    )


def sum_parts(parts, residual, heads):
    return kernel_call(
        sum_body, (shape((heads, *parts.shape[1:]), bf16),), [], parts, residual
    )[0]


def run_experts(first, x, chosen, marks, gain, router, gate, up, down):
    count, size, _ = x.shape
    return kernel_call(
        expert_body,
        (shape(x.shape, bf16), shape((size, LANES), f32)),
        [
            pltpu.VMEM((count * size, LANES), f32),
            pltpu.VMEM((size // 2, 2 * count, LANES), f32),
            pltpu.VMEM(down.shape, bf16),
            pltpu.SemaphoreType.DMA((down.shape[0],)),
        ],
        first, x, chosen, marks, gain, router, gate, up, down, scalars=1, hbm=(8,),
    )


def add_parts(parts, hidden):
    size = parts.shape[1]
    return kernel_call(
        final_body,
        (shape((2, size // 2 * LANES), f32),),
        [pltpu.VMEM((size, LANES), f32)],
        parts, hidden,
    )[0]


def chosen_lines(ids):
    mask = jnp.any(ids[..., None] == jnp.arange(LANES, dtype=jnp.int32), 1)
    return mask.astype(f32)


def layer(
    queries,
    shared_prefix_keys,
    shared_prefix_values,
    row_suffix_keys,
    row_suffix_values,
    suffix_lengths,
    residual,
    out_weight,
    norm_gain,
    router_weight,
    gate_weights,
    up_weights,
    down_weights,
    expert_ids,
):
    heads = lax.axis_size("head")
    dests = lax.axis_size("grp")
    block = lax.axis_index("grp").astype(jnp.int32).reshape(1)
    expert = (lax.axis_index("head") * gate_weights.shape[0]).astype(jnp.int32).reshape(1)
    send, own, marks = prefix_attention(
        block, expert, queries[0], shared_prefix_keys[0], shared_prefix_values[0], dests
    )
    arrived = exchange(send, "grp")
    near = heads // SPREAD
    place = (lax.axis_index("head") // near).astype(jnp.int32).reshape(1)
    pieces = list(pack_weights(place, out_weight, residual[0]))
    for s in range(1, SPREAD):
        ring = [(h, (h + s * near) % heads) for h in range(heads)]
        pieces[s] = lax.ppermute(pieces[s], "head", ring)
    suffix, stats = fill_window(
        suffix_lengths,
        own,
        row_suffix_keys.reshape(-1, row_suffix_keys.shape[-1]),
        row_suffix_values.reshape(-1, row_suffix_values.shape[-1]),
    )
    chosen = chosen_lines(expert_ids[0])
    attn, router, up = merge_parts(
        arrived, suffix, stats, chosen, router_weight.T, up_weights
    )
    attn = exchange(attn.reshape(heads, DEST_ROWS, HEAD_SIZE), "head")
    parts, chosen, residual_lines = project(
        place, attn.reshape(heads * DEST_ROWS, HEAD_SIZE), pieces
    )
    groups = [[y * near + n for n in range(near)] for y in range(SPREAD)]
    parts = exchange(parts, "head", groups)
    x = exchange(sum_parts(parts, residual_lines, heads), "head")
    made, hidden = run_experts(
        expert, x, chosen, marks, norm_gain[None], router, gate_weights, up, down_weights
    )
    return add_parts(exchange(made, "head"), hidden)[None]


def solution(mesh):
    return jax.shard_map(
        layer,
        mesh=mesh,
        in_specs=(
            P("head", None, None),
            P("head", "grp", None),
            P("head", "grp", None),
            P("head", "grp", None, None),
            P("head", "grp", None, None),
            P("head", "grp"),
            P("head", "grp", None),
            P("head", None),
            P(),
            P(),
            P("head", None, None),
            P("head", None, None),
            P("head", None, None),
            P("head", "grp", None),
        ),
        out_specs=P("head", "grp", None),
        check_vma=False,
    )
```

```python
import math

import jax
import jax.numpy as jnp
from jax import lax
from jax.experimental import pallas as pl
from jax.experimental.pallas import tpu as pltpu
from jax.sharding import PartitionSpec as P


QUERY_HEADS = 32
KEY_VALUE_HEADS = 4
HEAD_SIZE = 128
GROUP = QUERY_HEADS // KEY_VALUE_HEADS
LANES = 128
STAT_ROWS = 8
DEST_ROWS = 16
SPREAD = 4
EXPERTS_HERE = 2
EXTRA_ROWS = 8

masked_score = -1e30
norm_epsilon = 1e-06
score_scale = 1.0 / math.sqrt(HEAD_SIZE)
f32 = jnp.float32
bf16 = jnp.bfloat16
INTERPRET = False


def exchange(x, axis, groups=None):
    return lax.all_to_all(
        x, axis, split_axis=0, concat_axis=0, tiled=True, axis_index_groups=groups
    )


def kernel_call(body, outs, scratch, *args, hbm=(), hbm_outs=()):
    vmem = pl.BlockSpec(memory_space=pltpu.VMEM)
    raw = pl.BlockSpec(memory_space=pltpu.HBM)
    specs = [raw if i in hbm else vmem for i in range(len(args))]
    args = [
        pltpu.with_memory_space_constraint(a, pltpu.HBM) if i in hbm else a
        for i, a in enumerate(args)
    ]
    return pl.pallas_call(
        body,
        out_shape=outs,
        in_specs=specs,
        out_specs=tuple(raw if i in hbm_outs else vmem for i in range(len(outs))),
        scratch_shapes=scratch,
        compiler_params=pltpu.CompilerParams(vmem_limit_bytes=16 << 20),
        interpret=INTERPRET,
    )(*args)


def shape(dims, dtype):
    return jax.ShapeDtypeStruct(dims, dtype)


def head_columns(k):
    return slice(k * HEAD_SIZE, (k + 1) * HEAD_SIZE)


def dot_last(a, b):
    return lax.dot_general(a, b, (((1,), (1,)), ((), ())), preferred_element_type=f32)


def dot_first(a, b):
    return lax.dot_general(a, b, (((0,), (0,)), ((), ())), preferred_element_type=f32)


def start_copy(source, target, sem):
    copy = pltpu.make_async_copy(source, target, sem)
    copy.start()
    return copy


def prefix_body(
    q_hbm, k_hbm, v_hbm, out_hbm, own_ref, mark_ref,
    q_in, k_in, v_in, q_rows, stats, rests, made, in_sems, out_sems,
):
    rows = q_hbm.shape[0]
    dests = out_hbm.shape[0]
    per_dest = rows * GROUP // dests
    width = rows * GROUP
    wide = GROUP * HEAD_SIZE
    keys = start_copy(k_hbm, k_in, in_sems.at[KEY_VALUE_HEADS])
    arrivals = [
        start_copy(q_hbm.at[:, k * wide : (k + 1) * wide], q_in.at[k], in_sems.at[k])
        for k in range(KEY_VALUE_HEADS)
    ]
    values = start_copy(v_hbm, v_in, in_sems.at[KEY_VALUE_HEADS + 1])
    stats[...] = jnp.zeros(stats.shape, f32)
    rests[...] = jnp.zeros(rests.shape, f32)
    lane = lax.broadcasted_iota(jnp.int32, mark_ref.shape, 1)
    row = lax.broadcasted_iota(jnp.int32, mark_ref.shape, 0)
    first = lax.axis_index("head") * EXPERTS_HERE
    mark_ref[...] = (lane == first + row).astype(f32)
    start = pl.multiple_of(lax.axis_index("grp") * per_dest, per_dest)
    departures = []
    for k in range(KEY_VALUE_HEADS):
        arrivals[k].wait()
        if k == 0:
            keys.wait()
        for j in range(GROUP):
            q_rows[k, pl.ds(j, rows, stride=GROUP), :] = q_in[k, :, head_columns(j)].astype(f32)
        mine = slice(k * per_dest, (k + 1) * per_dest)
        own_ref[mine, :] = q_rows[k, pl.ds(start, per_dest), :]
        scores = dot_last(k_in[:, head_columns(k)], q_rows[k].astype(bf16)) * score_scale
        top = jnp.max(scores, 0, keepdims=True)
        top_high = top.astype(bf16).astype(f32)
        top_low = (top - top_high).astype(bf16).astype(f32)
        terms = jnp.exp(scores - (top_high + top_low))
        mass = jnp.sum(terms, 0, keepdims=True)
        mass_high = mass.astype(bf16).astype(f32)
        stats[k : k + 1, 0:width] = top_high
        stats[4 + k : 5 + k, 0:width] = mass_high
        rests[k : k + 1, 0:width] = top_low
        rests[4 + k : 5 + k, 0:width] = mass - mass_high
        if k == 0:
            values.wait()
        weighted = dot_first(terms.astype(bf16), v_in[:, head_columns(k)])
        made[:, mine, :] = weighted.astype(bf16).reshape(dests, per_dest, HEAD_SIZE)
        departures.append(start_copy(made.at[:, mine, :], out_hbm.at[:, mine, :], out_sems.at[k]))
    held = stats[...]
    rest = pltpu.roll(rests[...], per_dest, 1)
    low = lax.broadcasted_iota(jnp.int32, (STAT_ROWS, LANES), 1) < per_dest
    last = slice(KEY_VALUE_HEADS * per_dest, KEY_VALUE_HEADS * per_dest + STAT_ROWS)
    for d in range(dests):
        at = slice(d * per_dest, d * per_dest + LANES)
        made[d, last, :] = jnp.where(low, held[:, at], rest[:, at]).astype(bf16)
    departures.append(
        start_copy(made.at[:, last, :], out_hbm.at[:, last, :], out_sems.at[KEY_VALUE_HEADS])
    )
    for copy in departures:
        copy.wait()


def place_of(heads):
    return lax.axis_index("head") // (heads // SPREAD)


def pack_body(weight_hbm, residual_hbm, *refs):
    outs, (weight, residual, extra, extras, sems) = refs[:SPREAD], refs[SPREAD:]
    depth, width = weight.shape[0], outs[0].shape[1]
    place = place_of(QUERY_HEADS)
    load = start_copy(weight_hbm, weight, sems.at[0])
    small = start_copy(residual_hbm, residual, sems.at[1])
    small.wait()
    copies = []
    starts = []
    for s in range(SPREAD):
        start = pl.multiple_of(((place + s) & (SPREAD - 1)) * width, width)
        starts.append(start)
        extra[...] = jnp.zeros(extra.shape, f32)
        extra[0:2, :] = residual[:, pl.ds(start, width)].astype(f32)
        extras[s] = extra[...].astype(bf16)
        copies.append(
            start_copy(extras.at[s], outs[s].at[depth : depth + EXTRA_ROWS, :], sems.at[2 + s])
        )
    load.wait()
    for s in range(SPREAD):
        piece = weight.at[:, pl.ds(starts[s], width)]
        copies.append(start_copy(piece, outs[s].at[0:depth, :], sems.at[2 + SPREAD + s]))
    for copy in copies:
        copy.wait()


def window_body(
    own_ref, length_hbm, k_hbm, v_hbm, out_ref, stat_ref, length_ref, k_ref, v_ref, sems
):
    pairs = ((length_hbm, length_ref), (k_hbm, k_ref), (v_hbm, v_ref))
    copies = [start_copy(a, b, sems.at[n]) for n, (a, b) in enumerate(pairs)]
    for copy in copies:
        copy.wait()
    suffix_attention(length_ref, own_ref, k_ref, v_ref, out_ref, stat_ref)


def suffix_attention(length_ref, own_ref, k_ref, v_ref, out_ref, stat_ref):
    per_dest = own_ref.shape[0] // KEY_VALUE_HEADS
    keys = k_ref.shape[0]
    half = keys // 2
    row = lax.broadcasted_iota(jnp.int32, (keys, per_dest), 0)
    lane = lax.broadcasted_iota(jnp.int32, (keys, per_dest), 1)
    second = row >= half
    limit = jnp.where(second, length_ref[:, 1:2] + half, length_ref[:, 0:1])
    inside = (second == (lane >= GROUP)) & (row < limit)
    stat_ref[...] = jnp.zeros(stat_ref.shape, f32)
    for k in range(KEY_VALUE_HEADS):
        q = own_ref[k * per_dest : (k + 1) * per_dest, :].astype(bf16)
        scores = dot_last(k_ref[:, head_columns(k)], q) * score_scale
        scores = jnp.where(inside, scores, masked_score)
        top = jnp.max(scores, 0, keepdims=True)
        terms = jnp.where(inside, jnp.exp(scores - top), 0.0)
        mass = jnp.sum(terms, 0, keepdims=True)
        stat_ref[k : k + 1, 0:per_dest] = top
        stat_ref[4 + k : 5 + k, 0:per_dest] = mass
        out_ref[k * per_dest : (k + 1) * per_dest, :] = dot_first(
            terms.astype(bf16), v_ref[:, head_columns(k)]
        )


def merge_body(
    suffix_ref, stat_ref, part_hbm, id_hbm, router_hbm, up_hbm,
    out_ref, router_ref, up_ref, part_ref, id_ref, rows, heads, sems,
):
    pairs = (
        (part_hbm, part_ref),
        (id_hbm, id_ref),
        (router_hbm, router_ref),
        (up_hbm, up_ref),
    )
    copies = [start_copy(a, b, sems.at[n]) for n, (a, b) in enumerate(pairs)]
    rows[...] = jnp.zeros(rows.shape, f32)
    copies[0].wait()
    sources = part_ref.shape[0]
    per_dest = suffix_ref.shape[0] // KEY_VALUE_HEADS
    first = KEY_VALUE_HEADS * per_dest
    held = [stat_ref[...]]
    for g in range(sources):
        both = part_ref[g, first : first + STAT_ROWS, :].astype(f32)
        held.append(both + pltpu.roll(both, LANES - per_dest, 1))
    top = held[0]
    for t in held[1:]:
        top = jnp.maximum(top, t)
    scales = [jnp.exp(t - top) for t in held]
    masses = [pltpu.roll(t, 4, 0) for t in held]
    total = scales[0] * masses[0]
    for s, m in zip(scales[1:], masses[1:]):
        total = total + s * m
    inverse = 1.0 / total
    scales = [s * inverse for s in scales]
    scales += [jnp.zeros((8, LANES), f32)] * (-len(scales) % 16)
    table = jnp.concatenate(scales, 0)
    turned = jnp.concatenate(
        [table[i : i + LANES].T[0:per_dest] for i in range(0, table.shape[0], LANES)], 1
    )
    for k in range(KEY_VALUE_HEADS):
        mine = slice(k * per_dest, (k + 1) * per_dest)
        mixed = turned[:, k : k + 1] * suffix_ref[mine, :]
        for g in range(sources):
            at = (g + 1) * 8 + k
            mixed = mixed + turned[:, at : at + 1] * part_ref[g, mine, :].astype(f32)
        for i in range(2):
            heads[i * QUERY_HEADS + k * GROUP : i * QUERY_HEADS + (k + 1) * GROUP, :] = mixed[
                i * GROUP : (i + 1) * GROUP
            ]
    near = QUERY_HEADS // SPREAD
    for y in range(SPREAD):
        for s in range(SPREAD):
            source = (y - s) % SPREAD * near
            for i in range(2):
                at = y * near * DEST_ROWS + i * SPREAD + s
                rows[pl.ds(at, near, stride=DEST_ROWS), :] = heads[
                    i * QUERY_HEADS + source : i * QUERY_HEADS + source + near, :
                ]
    copies[1].wait()
    lane = lax.broadcasted_iota(jnp.int32, (QUERY_HEADS, LANES), 1)
    for i in range(2):
        chosen = lane == id_ref[i : i + 1, 0:1]
        for n in range(1, id_ref.shape[1]):
            chosen = chosen | (lane == id_ref[i : i + 1, n : n + 1])
        line = chosen.astype(f32)
        rows[pl.ds(2 * SPREAD + i, QUERY_HEADS, stride=DEST_ROWS), :] = line
    out_ref[...] = rows[...].astype(bf16)
    for copy in copies[2:]:
        copy.wait()


def project_body(attn_ref, *refs):
    pieces, (out_ref, chosen_ref, residual_ref, rows, lines) = refs[:SPREAD], refs[SPREAD:]
    count = attn_ref.shape[0] // DEST_ROWS
    depth = pieces[0].shape[0] - EXTRA_ROWS
    near = count // SPREAD
    blocks = pieces[0].shape[1] // LANES
    rows[...] = attn_ref[...].astype(f32)
    for i in range(2):
        line = rows[pl.ds(2 * SPREAD + i, count, stride=DEST_ROWS), :]
        chosen_ref[i * count : (i + 1) * count, :] = line
    made = jnp.zeros((2 * count, blocks * LANES), f32)
    for s in range(SPREAD):
        attn = [rows[pl.ds(i * SPREAD + s, count, stride=DEST_ROWS), :] for i in range(2)]
        attn = jnp.concatenate(attn, 0).astype(bf16)
        made = made + jnp.dot(attn, pieces[s][0:depth, :], preferred_element_type=f32)
        extra = pieces[s][depth : depth + EXTRA_ROWS, :].astype(f32)
        source = (place_of(count) + SPREAD - s) & (SPREAD - 1)
        for i in range(2):
            for c in range(blocks):
                residual_ref[pl.ds(c * 2 * SPREAD + i * SPREAD + source, 1), :] = extra[
                    i : i + 1, c * LANES : (c + 1) * LANES
                ]
    for c in range(blocks):
        lines[c] = made[:, c * LANES : (c + 1) * LANES]
    for n in range(near):
        parts = [lines[c, pl.ds(n, 2 * SPREAD, stride=near), :] for c in range(blocks)]
        out_ref[n] = jnp.concatenate(parts, 0).astype(bf16)


def spread_rows(made, lines, count, blocks):
    for i in range(2):
        for c in range(blocks):
            lines[pl.ds(i * blocks + c, count, stride=2 * blocks), :] = made[
                i * count : (i + 1) * count, c * LANES : (c + 1) * LANES
            ]


def sum_body(part_ref, residual_ref, out_ref):
    hidden = residual_ref[...]
    for n in range(part_ref.shape[0]):
        hidden = hidden + part_ref[n].astype(f32)
    hidden = hidden.astype(bf16)
    for h in range(out_ref.shape[0]):
        out_ref[h] = hidden


def expert_body(
    x_ref, chosen_ref, mark_ref, gain_ref, router_ref, gate, up, down_hbm,
    out_ref, hidden_ref, lines, x_rows, down, sems,
):
    experts = gate.shape[0]
    copies = [start_copy(down_hbm.at[e], down.at[e], sems.at[e]) for e in range(experts)]
    count, size, _ = x_ref.shape
    near = count // SPREAD
    pairs = 2 * SPREAD
    blocks = size // pairs
    own = lax.axis_index("head")
    far = own // near
    lines[...] = x_ref[...].astype(f32).reshape(lines.shape)
    for y in range(SPREAD):
        for c in range(blocks):
            for n in range(near):
                at = (y * near + n) * size + c * pairs
                x_rows[y * blocks + c, pl.ds(n, pairs, stride=near), :] = lines[at : at + pairs, :]
            for i in range(2):
                at = (y * near + own - far * near) * size + c * pairs + i * SPREAD + far
                to = (i * SPREAD + y) * blocks + c
                hidden_ref[to : to + 1, :] = lines[pl.ds(at, 1), :]
    hidden = jnp.concatenate([x_rows[c] for c in range(SPREAD * blocks)], 1)
    mean_square = jnp.sum(hidden * hidden, 1, keepdims=True) / hidden.shape[1]
    x = (hidden * lax.rsqrt(mean_square + norm_epsilon) * gain_ref[...]).astype(bf16)
    logits = dot_last(x, router_ref[...])
    expo = jnp.where(chosen_ref[:, 0 : logits.shape[1]] > 0.5, jnp.exp(logits), 0.0)
    mass = jnp.sum(expo, 1, keepdims=True)
    mixed = jnp.zeros((2 * count, down.shape[2]), f32)
    for e in range(experts):
        gate_out = jnp.dot(x, gate[e], preferred_element_type=f32)
        up_out = jnp.dot(x, up[e], preferred_element_type=f32)
        act = (gate_out / (1.0 + jnp.exp(-gate_out)) * up_out).astype(bf16)
        copies[e].wait()
        made = jnp.dot(act, down[e], preferred_element_type=f32).astype(bf16).astype(f32)
        mark = mark_ref[e : e + 1, 0 : expo.shape[1]] > 0.5
        mine = jnp.sum(jnp.where(mark, expo, 0.0), 1, keepdims=True)
        mixed = mixed + (mine / mass) * made
    spread_rows(mixed, lines, count, size // 2)
    out_ref[...] = lines[...].astype(bf16).reshape(count, size, LANES)


def final_body(part_ref, hidden_ref, out_ref, lines):
    sources, size, _ = part_ref.shape
    blocks = size // 2
    total = part_ref[0].astype(f32)
    for s in range(1, sources):
        total = total + part_ref[s].astype(f32)
    lines[...] = hidden_ref[...] + total
    for c in range(blocks):
        out_ref[:, c * LANES : (c + 1) * LANES] = lines[pl.ds(c, 2, stride=blocks), :]


def prefix_attention(q, k, v, dests):
    rows = q.shape[0]
    per_dest = rows * GROUP // dests
    send = (dests, KEY_VALUE_HEADS * per_dest + STAT_ROWS, HEAD_SIZE)
    padded = (rows * GROUP // LANES + 1) * LANES
    made, own, marks = kernel_call(
        prefix_body,
        (
            pltpu.HBM(send, bf16),
            shape((KEY_VALUE_HEADS * per_dest, HEAD_SIZE), f32),
            shape((8, LANES), f32),
        ),
        [
            pltpu.VMEM((KEY_VALUE_HEADS, rows, GROUP * HEAD_SIZE), bf16),
            pltpu.VMEM(k.shape, bf16),
            pltpu.VMEM(v.shape, bf16),
            pltpu.VMEM((KEY_VALUE_HEADS, rows * GROUP, HEAD_SIZE), f32),
            pltpu.VMEM((STAT_ROWS, padded), f32),
            pltpu.VMEM((STAT_ROWS, padded), f32),
            pltpu.VMEM(send, bf16),
            pltpu.SemaphoreType.DMA((KEY_VALUE_HEADS + 2,)),
            pltpu.SemaphoreType.DMA((KEY_VALUE_HEADS + 1,)),
        ],
        q, k, v, hbm=(0, 1, 2), hbm_outs=(0,),
    )
    return made, own, marks


def pack_weights(weight, residual):
    width = weight.shape[1] // SPREAD
    dims = (weight.shape[0] + EXTRA_ROWS, width)
    return kernel_call(
        pack_body,
        tuple(pltpu.HBM(dims, bf16) for _ in range(SPREAD)),
        [
            pltpu.VMEM(weight.shape, bf16),
            pltpu.VMEM(residual.shape, bf16),
            pltpu.VMEM((EXTRA_ROWS, width), f32),
            pltpu.VMEM((SPREAD, EXTRA_ROWS, width), bf16),
            pltpu.SemaphoreType.DMA((2 + 2 * SPREAD,)),
        ],
        weight, residual, hbm=(0, 1), hbm_outs=range(SPREAD),
    )


def fill_window(lengths, own, k, v):
    return kernel_call(
        window_body,
        (shape(own.shape, f32), shape((STAT_ROWS, LANES), f32)),
        [
            pltpu.VMEM(lengths.shape, jnp.int32),
            pltpu.VMEM(k.shape, bf16),
            pltpu.VMEM(v.shape, bf16),
            pltpu.SemaphoreType.DMA((3,)),
        ],
        own, lengths, k, v, hbm=(1, 2, 3),
    )


def merge_parts(suffix, stats, parts, ids, *weights):
    dims = (QUERY_HEADS * DEST_ROWS, HEAD_SIZE)
    return kernel_call(
        merge_body,
        (shape(dims, bf16), *(shape(w.shape, bf16) for w in weights)),
        [
            pltpu.VMEM(parts.shape, bf16),
            pltpu.VMEM(ids.shape, jnp.int32),
            pltpu.VMEM(dims, f32),
            pltpu.VMEM((2 * QUERY_HEADS, HEAD_SIZE), f32),
            pltpu.SemaphoreType.DMA((2 + len(weights),)),
        ],
        suffix, stats, parts, ids, *weights, hbm=range(2, 4 + len(weights)),
    )


def project(attn, pieces):
    count = attn.shape[0] // DEST_ROWS
    near, blocks = count // SPREAD, pieces[0].shape[1] // LANES
    size = 2 * SPREAD * blocks
    return kernel_call(
        project_body,
        (
            shape((near, size, LANES), bf16),
            shape((2 * count, LANES), f32),
            shape((size, LANES), f32),
        ),
        [pltpu.VMEM(attn.shape, f32), pltpu.VMEM((blocks, 2 * count, LANES), f32)],
        attn, *pieces,
    )


def sum_parts(parts, residual, heads):
    return kernel_call(
        sum_body, (shape((heads, *parts.shape[1:]), bf16),), [], parts, residual
    )[0]


def run_experts(x, chosen, marks, gain, router, gate, up, down):
    count, size, _ = x.shape
    return kernel_call(
        expert_body,
        (shape(x.shape, bf16), shape((size, LANES), f32)),
        [
            pltpu.VMEM((count * size, LANES), f32),
            pltpu.VMEM((size // 2, 2 * count, LANES), f32),
            pltpu.VMEM(down.shape, bf16),
            pltpu.SemaphoreType.DMA((down.shape[0],)),
        ],
        x, chosen, marks, gain, router, gate, up, down, hbm=(7,),
    )


def add_parts(parts, hidden):
    size = parts.shape[1]
    return kernel_call(
        final_body,
        (shape((2, size // 2 * LANES), f32),),
        [pltpu.VMEM((size, LANES), f32)],
        parts, hidden,
    )[0]


def layer(
    queries,
    shared_prefix_keys,
    shared_prefix_values,
    row_suffix_keys,
    row_suffix_values,
    suffix_lengths,
    residual,
    out_weight,
    norm_gain,
    router_weight,
    gate_weights,
    up_weights,
    down_weights,
    expert_ids,
):
    heads = lax.axis_size("head")
    dests = lax.axis_size("grp")
    send, own, marks = prefix_attention(
        queries[0], shared_prefix_keys[0], shared_prefix_values[0], dests
    )
    arrived = exchange(send, "grp")
    near = heads // SPREAD
    pieces = list(pack_weights(out_weight, residual[0]))
    for s in range(1, SPREAD):
        ring = [(h, (h + s * near) % heads) for h in range(heads)]
        pieces[s] = lax.ppermute(pieces[s], "head", ring)
        pieces[s] = pltpu.with_memory_space_constraint(pieces[s], pltpu.HBM)
    suffix, stats = fill_window(
        suffix_lengths,
        own,
        row_suffix_keys.reshape(-1, row_suffix_keys.shape[-1]),
        row_suffix_values.reshape(-1, row_suffix_values.shape[-1]),
    )
    attn, router, up = merge_parts(
        suffix, stats, arrived, expert_ids[0], router_weight.T, up_weights
    )
    attn = exchange(attn.reshape(heads, DEST_ROWS, HEAD_SIZE), "head")
    parts, chosen, residual_lines = project(
        attn.reshape(heads * DEST_ROWS, HEAD_SIZE), pieces
    )
    groups = [[y * near + n for n in range(near)] for y in range(SPREAD)]
    parts = exchange(parts, "head", groups)
    x = exchange(sum_parts(parts, residual_lines, heads), "head")
    made, hidden = run_experts(
        x, chosen, marks, norm_gain[None], router, gate_weights, up, down_weights
    )
    return add_parts(exchange(made, "head"), hidden)[None]


def solution(mesh):
    return jax.shard_map(
        layer,
        mesh=mesh,
        in_specs=(
            P("head", None, None),
            P("head", "grp", None),
            P("head", "grp", None),
            P("head", "grp", None, None),
            P("head", "grp", None, None),
            P("head", "grp"),
            P("head", "grp", None),
            P("head", None),
            P(),
            P(),
            P("head", None, None),
            P("head", None, None),
            P("head", None, None),
            P("head", "grp", None),
        ),
        out_specs=P("head", "grp", None),
        check_vma=False,
    )
```

```python
import math

import jax
import jax.numpy as jnp
from jax import lax
from jax.experimental import pallas as pl
from jax.experimental.pallas import tpu as pltpu
from jax.sharding import PartitionSpec as P


QUERY_HEADS = 32
KEY_VALUE_HEADS = 4
HEAD_SIZE = 128
GROUP = QUERY_HEADS // KEY_VALUE_HEADS
LANES = 128
STAT_ROWS = 8
DEST_ROWS = 16
SPREAD = 4
EXPERTS_HERE = 2
EXTRA_ROWS = 8

masked_score = -1e30
norm_epsilon = 1e-06
score_scale = 1.0 / math.sqrt(HEAD_SIZE)
f32 = jnp.float32
bf16 = jnp.bfloat16
INTERPRET = False


def exchange(x, axis, groups=None):
    return lax.all_to_all(
        x, axis, split_axis=0, concat_axis=0, tiled=True, axis_index_groups=groups
    )


def kernel_call(body, outs, scratch, *args, hbm=(), hbm_outs=()):
    vmem = pl.BlockSpec(memory_space=pltpu.VMEM)
    raw = pl.BlockSpec(memory_space=pltpu.HBM)
    specs = [raw if i in hbm else vmem for i in range(len(args))]
    args = [
        pltpu.with_memory_space_constraint(a, pltpu.HBM) if i in hbm else a
        for i, a in enumerate(args)
    ]
    return pl.pallas_call(
        body,
        out_shape=outs,
        in_specs=specs,
        out_specs=tuple(raw if i in hbm_outs else vmem for i in range(len(outs))),
        scratch_shapes=scratch,
        compiler_params=pltpu.CompilerParams(vmem_limit_bytes=16 << 20),
        interpret=INTERPRET,
    )(*args)


def shape(dims, dtype):
    return jax.ShapeDtypeStruct(dims, dtype)


def head_columns(k):
    return slice(k * HEAD_SIZE, (k + 1) * HEAD_SIZE)


def dot_last(a, b):
    return lax.dot_general(a, b, (((1,), (1,)), ((), ())), preferred_element_type=f32)


def dot_first(a, b):
    return lax.dot_general(a, b, (((0,), (0,)), ((), ())), preferred_element_type=f32)


def start_copy(source, target, sem):
    copy = pltpu.make_async_copy(source, target, sem)
    copy.start()
    return copy


def prefix_body(
    q_hbm, k_hbm, v_hbm, out_hbm, own_ref, mark_ref,
    q_in, k_in, v_in, q_rows, stats, rests, made, in_sems, out_sems,
):
    rows = q_hbm.shape[0]
    dests = out_hbm.shape[0]
    per_dest = rows * GROUP // dests
    width = rows * GROUP
    wide = GROUP * HEAD_SIZE
    keys = start_copy(k_hbm, k_in, in_sems.at[KEY_VALUE_HEADS])
    arrivals = [
        start_copy(q_hbm.at[:, k * wide : (k + 1) * wide], q_in.at[k], in_sems.at[k])
        for k in range(KEY_VALUE_HEADS)
    ]
    values = start_copy(v_hbm, v_in, in_sems.at[KEY_VALUE_HEADS + 1])
    stats[...] = jnp.zeros(stats.shape, f32)
    rests[...] = jnp.zeros(rests.shape, f32)
    lane = lax.broadcasted_iota(jnp.int32, mark_ref.shape, 1)
    row = lax.broadcasted_iota(jnp.int32, mark_ref.shape, 0)
    first = lax.axis_index("head") * EXPERTS_HERE
    mark_ref[...] = (lane == first + row).astype(f32)
    start = pl.multiple_of(lax.axis_index("grp") * per_dest, per_dest)
    departures = []
    for k in range(KEY_VALUE_HEADS):
        arrivals[k].wait()
        if k == 0:
            keys.wait()
        for j in range(GROUP):
            q_rows[k, pl.ds(j, rows, stride=GROUP), :] = q_in[k, :, head_columns(j)].astype(f32)
        mine = slice(k * per_dest, (k + 1) * per_dest)
        own_ref[mine, :] = q_rows[k, pl.ds(start, per_dest), :]
        scores = dot_last(k_in[:, head_columns(k)], q_rows[k].astype(bf16)) * score_scale
        top = jnp.max(scores, 0, keepdims=True)
        top_high = top.astype(bf16).astype(f32)
        top_low = (top - top_high).astype(bf16).astype(f32)
        terms = jnp.exp(scores - (top_high + top_low))
        mass = jnp.sum(terms, 0, keepdims=True)
        mass_high = mass.astype(bf16).astype(f32)
        stats[k : k + 1, 0:width] = top_high
        stats[4 + k : 5 + k, 0:width] = mass_high
        rests[k : k + 1, 0:width] = top_low
        rests[4 + k : 5 + k, 0:width] = mass - mass_high
        if k == 0:
            values.wait()
        weighted = dot_first(terms.astype(bf16), v_in[:, head_columns(k)])
        made[:, mine, :] = weighted.astype(bf16).reshape(dests, per_dest, HEAD_SIZE)
        departures.append(start_copy(made.at[:, mine, :], out_hbm.at[:, mine, :], out_sems.at[k]))
    held = stats[...]
    rest = pltpu.roll(rests[...], per_dest, 1)
    low = lax.broadcasted_iota(jnp.int32, (STAT_ROWS, LANES), 1) < per_dest
    last = slice(KEY_VALUE_HEADS * per_dest, KEY_VALUE_HEADS * per_dest + STAT_ROWS)
    for d in range(dests):
        at = slice(d * per_dest, d * per_dest + LANES)
        made[d, last, :] = jnp.where(low, held[:, at], rest[:, at]).astype(bf16)
    departures.append(
        start_copy(made.at[:, last, :], out_hbm.at[:, last, :], out_sems.at[KEY_VALUE_HEADS])
    )
    for copy in departures:
        copy.wait()


def place_of(heads):
    return lax.axis_index("head") // (heads // SPREAD)


def pack_body(weight_hbm, residual_hbm, *refs):
    outs, (residual, extra, extras, sems) = refs[:SPREAD], refs[SPREAD:]
    depth, width = weight_hbm.shape[0], outs[0].shape[1]
    place = place_of(QUERY_HEADS)
    small = start_copy(residual_hbm, residual, sems.at[0])
    starts = [
        pl.multiple_of(((place + s) & (SPREAD - 1)) * width, width) for s in range(SPREAD)
    ]
    copies = [
        start_copy(
            weight_hbm.at[:, pl.ds(start, width)], outs[s].at[0:depth, :], sems.at[1 + s]
        )
        for s, start in enumerate(starts)
    ]
    extra[...] = jnp.zeros(extra.shape, f32)
    small.wait()
    for s, start in enumerate(starts):
        extra[0:2, :] = residual[:, pl.ds(start, width)].astype(f32)
        extras[s] = extra[...].astype(bf16)
        target = outs[s].at[depth : depth + EXTRA_ROWS, :]
        copies.append(start_copy(extras.at[s], target, sems.at[1 + SPREAD + s]))
    for copy in copies:
        copy.wait()


def window_body(
    own_ref, length_hbm, k_hbm, v_hbm, out_ref, stat_ref, length_ref, k_ref, v_ref, sems
):
    pairs = ((length_hbm, length_ref), (k_hbm, k_ref), (v_hbm, v_ref))
    copies = [start_copy(a, b, sems.at[n]) for n, (a, b) in enumerate(pairs)]
    for copy in copies:
        copy.wait()
    suffix_attention(length_ref, own_ref, k_ref, v_ref, out_ref, stat_ref)


def suffix_attention(length_ref, own_ref, k_ref, v_ref, out_ref, stat_ref):
    per_dest = own_ref.shape[0] // KEY_VALUE_HEADS
    keys = k_ref.shape[0]
    half = keys // 2
    row = lax.broadcasted_iota(jnp.int32, (keys, per_dest), 0)
    lane = lax.broadcasted_iota(jnp.int32, (keys, per_dest), 1)
    second = row >= half
    limit = jnp.where(second, length_ref[:, 1:2] + half, length_ref[:, 0:1])
    inside = (second == (lane >= GROUP)) & (row < limit)
    stat_ref[...] = jnp.zeros(stat_ref.shape, f32)
    for k in range(KEY_VALUE_HEADS):
        q = own_ref[k * per_dest : (k + 1) * per_dest, :].astype(bf16)
        scores = dot_last(k_ref[:, head_columns(k)], q) * score_scale
        scores = jnp.where(inside, scores, masked_score)
        top = jnp.max(scores, 0, keepdims=True)
        terms = jnp.where(inside, jnp.exp(scores - top), 0.0)
        mass = jnp.sum(terms, 0, keepdims=True)
        stat_ref[k : k + 1, 0:per_dest] = top
        stat_ref[4 + k : 5 + k, 0:per_dest] = mass
        out_ref[k * per_dest : (k + 1) * per_dest, :] = dot_first(
            terms.astype(bf16), v_ref[:, head_columns(k)]
        )


def merge_body(part_ref, suffix_ref, stat_ref, *refs):
    count = (len(refs) - 6) // 2
    sources, (out_ref, *targets) = refs[: 1 + count], refs[1 + count : 2 + 2 * count]
    id_ref, rows, heads, sems = refs[2 + 2 * count :]
    pairs = list(zip(sources, (id_ref, *targets)))
    copies = [start_copy(a, b, sems.at[n]) for n, (a, b) in enumerate(pairs)]
    rows[...] = jnp.zeros(rows.shape, f32)
    part_count = part_ref.shape[0]
    per_dest = suffix_ref.shape[0] // KEY_VALUE_HEADS
    first = KEY_VALUE_HEADS * per_dest
    held = [stat_ref[...]]
    for g in range(part_count):
        both = part_ref[g, first : first + STAT_ROWS, :].astype(f32)
        held.append(both + pltpu.roll(both, LANES - per_dest, 1))
    top = held[0]
    for t in held[1:]:
        top = jnp.maximum(top, t)
    scales = [jnp.exp(t - top) for t in held]
    masses = [pltpu.roll(t, 4, 0) for t in held]
    total = scales[0] * masses[0]
    for s, m in zip(scales[1:], masses[1:]):
        total = total + s * m
    inverse = 1.0 / total
    scales = [s * inverse for s in scales]
    scales += [jnp.zeros((8, LANES), f32)] * (-len(scales) % 16)
    table = jnp.concatenate(scales, 0)
    turned = jnp.concatenate(
        [table[i : i + LANES].T[0:per_dest] for i in range(0, table.shape[0], LANES)], 1
    )
    for k in range(KEY_VALUE_HEADS):
        mine = slice(k * per_dest, (k + 1) * per_dest)
        mixed = turned[:, k : k + 1] * suffix_ref[mine, :]
        for g in range(part_count):
            at = (g + 1) * 8 + k
            mixed = mixed + turned[:, at : at + 1] * part_ref[g, mine, :].astype(f32)
        for i in range(2):
            heads[i * QUERY_HEADS + k * GROUP : i * QUERY_HEADS + (k + 1) * GROUP, :] = mixed[
                i * GROUP : (i + 1) * GROUP
            ]
    near = QUERY_HEADS // SPREAD
    for y in range(SPREAD):
        for s in range(SPREAD):
            source = (y - s) % SPREAD * near
            for i in range(2):
                at = y * near * DEST_ROWS + i * SPREAD + s
                rows[pl.ds(at, near, stride=DEST_ROWS), :] = heads[
                    i * QUERY_HEADS + source : i * QUERY_HEADS + source + near, :
                ]
    copies[0].wait()
    lane = lax.broadcasted_iota(jnp.int32, (QUERY_HEADS, LANES), 1)
    for i in range(2):
        chosen = lane == id_ref[i : i + 1, 0:1]
        for n in range(1, id_ref.shape[1]):
            chosen = chosen | (lane == id_ref[i : i + 1, n : n + 1])
        line = chosen.astype(f32)
        rows[pl.ds(2 * SPREAD + i, QUERY_HEADS, stride=DEST_ROWS), :] = line
    out_ref[...] = rows[...].astype(bf16)
    for copy in copies[1:]:
        copy.wait()


def project_body(attn_ref, *refs):
    pieces, (out_ref, chosen_ref, residual_ref, rows, lines) = refs[:SPREAD], refs[SPREAD:]
    count = attn_ref.shape[0] // DEST_ROWS
    depth = pieces[0].shape[0] - EXTRA_ROWS
    near = count // SPREAD
    blocks = pieces[0].shape[1] // LANES
    rows[...] = attn_ref[...].astype(f32)
    for i in range(2):
        line = rows[pl.ds(2 * SPREAD + i, count, stride=DEST_ROWS), :]
        chosen_ref[i * count : (i + 1) * count, :] = line
    made = jnp.zeros((2 * count, blocks * LANES), f32)
    for s in range(SPREAD):
        attn = [rows[pl.ds(i * SPREAD + s, count, stride=DEST_ROWS), :] for i in range(2)]
        attn = jnp.concatenate(attn, 0).astype(bf16)
        made = made + jnp.dot(attn, pieces[s][0:depth, :], preferred_element_type=f32)
        extra = pieces[s][depth : depth + EXTRA_ROWS, :].astype(f32)
        source = (place_of(count) + SPREAD - s) & (SPREAD - 1)
        for i in range(2):
            for c in range(blocks):
                residual_ref[pl.ds(c * 2 * SPREAD + i * SPREAD + source, 1), :] = extra[
                    i : i + 1, c * LANES : (c + 1) * LANES
                ]
    for c in range(blocks):
        lines[c] = made[:, c * LANES : (c + 1) * LANES]
    for n in range(near):
        parts = [lines[c, pl.ds(n, 2 * SPREAD, stride=near), :] for c in range(blocks)]
        out_ref[n] = jnp.concatenate(parts, 0).astype(bf16)


def spread_rows(made, lines, count, blocks):
    for i in range(2):
        for c in range(blocks):
            lines[pl.ds(i * blocks + c, count, stride=2 * blocks), :] = made[
                i * count : (i + 1) * count, c * LANES : (c + 1) * LANES
            ]


def sum_body(part_ref, residual_ref, out_ref):
    hidden = residual_ref[...]
    for n in range(part_ref.shape[0]):
        hidden = hidden + part_ref[n].astype(f32)
    hidden = hidden.astype(bf16)
    for h in range(out_ref.shape[0]):
        out_ref[h] = hidden


def expert_body(
    x_ref, chosen_ref, mark_ref, gain_ref, router_ref, gate, up, down_hbm,
    out_ref, hidden_ref, lines, x_rows, down, sems,
):
    experts = gate.shape[0]
    copies = [start_copy(down_hbm.at[e], down.at[e], sems.at[e]) for e in range(experts)]
    count, size, _ = x_ref.shape
    near = count // SPREAD
    pairs = 2 * SPREAD
    blocks = size // pairs
    own = lax.axis_index("head")
    far = own // near
    lines[...] = x_ref[...].astype(f32).reshape(lines.shape)
    for y in range(SPREAD):
        for c in range(blocks):
            for n in range(near):
                at = (y * near + n) * size + c * pairs
                x_rows[y * blocks + c, pl.ds(n, pairs, stride=near), :] = lines[at : at + pairs, :]
            for i in range(2):
                at = (y * near + own - far * near) * size + c * pairs + i * SPREAD + far
                to = (i * SPREAD + y) * blocks + c
                hidden_ref[to : to + 1, :] = lines[pl.ds(at, 1), :]
    hidden = jnp.concatenate([x_rows[c] for c in range(SPREAD * blocks)], 1)
    mean_square = jnp.sum(hidden * hidden, 1, keepdims=True) / hidden.shape[1]
    x = (hidden * lax.rsqrt(mean_square + norm_epsilon) * gain_ref[...]).astype(bf16)
    logits = dot_last(x, router_ref[...])
    expo = jnp.where(chosen_ref[:, 0 : logits.shape[1]] > 0.5, jnp.exp(logits), 0.0)
    mass = jnp.sum(expo, 1, keepdims=True)
    mixed = jnp.zeros((2 * count, down.shape[2]), f32)
    for e in range(experts):
        gate_out = jnp.dot(x, gate[e], preferred_element_type=f32)
        up_out = jnp.dot(x, up[e], preferred_element_type=f32)
        act = (gate_out / (1.0 + jnp.exp(-gate_out)) * up_out).astype(bf16)
        copies[e].wait()
        made = jnp.dot(act, down[e], preferred_element_type=f32).astype(bf16).astype(f32)
        mark = mark_ref[e : e + 1, 0 : expo.shape[1]] > 0.5
        mine = jnp.sum(jnp.where(mark, expo, 0.0), 1, keepdims=True)
        mixed = mixed + (mine / mass) * made
    spread_rows(mixed, lines, count, size // 2)
    out_ref[...] = lines[...].astype(bf16).reshape(count, size, LANES)


def final_body(part_ref, hidden_ref, out_ref, lines):
    sources, size, _ = part_ref.shape
    blocks = size // 2
    total = part_ref[0].astype(f32)
    for s in range(1, sources):
        total = total + part_ref[s].astype(f32)
    lines[...] = hidden_ref[...] + total
    for c in range(blocks):
        out_ref[:, c * LANES : (c + 1) * LANES] = lines[pl.ds(c, 2, stride=blocks), :]


def prefix_attention(q, k, v, dests):
    rows = q.shape[0]
    per_dest = rows * GROUP // dests
    send = (dests, KEY_VALUE_HEADS * per_dest + STAT_ROWS, HEAD_SIZE)
    padded = (rows * GROUP // LANES + 1) * LANES
    made, own, marks = kernel_call(
        prefix_body,
        (
            pltpu.HBM(send, bf16),
            shape((KEY_VALUE_HEADS * per_dest, HEAD_SIZE), f32),
            shape((8, LANES), f32),
        ),
        [
            pltpu.VMEM((KEY_VALUE_HEADS, rows, GROUP * HEAD_SIZE), bf16),
            pltpu.VMEM(k.shape, bf16),
            pltpu.VMEM(v.shape, bf16),
            pltpu.VMEM((KEY_VALUE_HEADS, rows * GROUP, HEAD_SIZE), f32),
            pltpu.VMEM((STAT_ROWS, padded), f32),
            pltpu.VMEM((STAT_ROWS, padded), f32),
            pltpu.VMEM(send, bf16),
            pltpu.SemaphoreType.DMA((KEY_VALUE_HEADS + 2,)),
            pltpu.SemaphoreType.DMA((KEY_VALUE_HEADS + 1,)),
        ],
        q, k, v, hbm=(0, 1, 2), hbm_outs=(0,),
    )
    return made, own, marks


def pack_weights(weight, residual):
    width = weight.shape[1] // SPREAD
    dims = (weight.shape[0] + EXTRA_ROWS, width)
    return kernel_call(
        pack_body,
        tuple(pltpu.HBM(dims, bf16) for _ in range(SPREAD)),
        [
            pltpu.VMEM(residual.shape, bf16),
            pltpu.VMEM((EXTRA_ROWS, width), f32),
            pltpu.VMEM((SPREAD, EXTRA_ROWS, width), bf16),
            pltpu.SemaphoreType.DMA((1 + 2 * SPREAD,)),
        ],
        weight, residual, hbm=(0, 1), hbm_outs=range(SPREAD),
    )


def fill_window(lengths, own, k, v):
    return kernel_call(
        window_body,
        (shape(own.shape, f32), shape((STAT_ROWS, LANES), f32)),
        [
            pltpu.VMEM(lengths.shape, jnp.int32),
            pltpu.VMEM(k.shape, bf16),
            pltpu.VMEM(v.shape, bf16),
            pltpu.SemaphoreType.DMA((3,)),
        ],
        own, lengths, k, v, hbm=(1, 2, 3),
    )


def merge_parts(parts, suffix, stats, ids, *weights):
    dims = (QUERY_HEADS * DEST_ROWS, HEAD_SIZE)
    return kernel_call(
        merge_body,
        (shape(dims, bf16), *(shape(w.shape, bf16) for w in weights)),
        [
            pltpu.VMEM(ids.shape, jnp.int32),
            pltpu.VMEM(dims, f32),
            pltpu.VMEM((2 * QUERY_HEADS, HEAD_SIZE), f32),
            pltpu.SemaphoreType.DMA((1 + len(weights),)),
        ],
        parts, suffix, stats, ids, *weights, hbm=range(3, 4 + len(weights)),
    )


def project(attn, pieces):
    count = attn.shape[0] // DEST_ROWS
    near, blocks = count // SPREAD, pieces[0].shape[1] // LANES
    size = 2 * SPREAD * blocks
    return kernel_call(
        project_body,
        (
            shape((near, size, LANES), bf16),
            shape((2 * count, LANES), f32),
            shape((size, LANES), f32),
        ),
        [pltpu.VMEM(attn.shape, f32), pltpu.VMEM((blocks, 2 * count, LANES), f32)],
        attn, *pieces,
    )


def sum_parts(parts, residual, heads):
    return kernel_call(
        sum_body, (shape((heads, *parts.shape[1:]), bf16),), [], parts, residual
    )[0]


def run_experts(x, chosen, marks, gain, router, gate, up, down):
    count, size, _ = x.shape
    return kernel_call(
        expert_body,
        (shape(x.shape, bf16), shape((size, LANES), f32)),
        [
            pltpu.VMEM((count * size, LANES), f32),
            pltpu.VMEM((size // 2, 2 * count, LANES), f32),
            pltpu.VMEM(down.shape, bf16),
            pltpu.SemaphoreType.DMA((down.shape[0],)),
        ],
        x, chosen, marks, gain, router, gate, up, down, hbm=(7,),
    )


def add_parts(parts, hidden):
    size = parts.shape[1]
    return kernel_call(
        final_body,
        (shape((2, size // 2 * LANES), f32),),
        [pltpu.VMEM((size, LANES), f32)],
        parts, hidden,
    )[0]


def layer(
    queries,
    shared_prefix_keys,
    shared_prefix_values,
    row_suffix_keys,
    row_suffix_values,
    suffix_lengths,
    residual,
    out_weight,
    norm_gain,
    router_weight,
    gate_weights,
    up_weights,
    down_weights,
    expert_ids,
):
    heads = lax.axis_size("head")
    dests = lax.axis_size("grp")
    send, own, marks = prefix_attention(
        queries[0], shared_prefix_keys[0], shared_prefix_values[0], dests
    )
    arrived = exchange(send, "grp")
    near = heads // SPREAD
    pieces = list(pack_weights(out_weight, residual[0]))
    for s in range(1, SPREAD):
        ring = [(h, (h + s * near) % heads) for h in range(heads)]
        pieces[s] = lax.ppermute(pieces[s], "head", ring)
    suffix, stats = fill_window(
        suffix_lengths,
        own,
        row_suffix_keys.reshape(-1, row_suffix_keys.shape[-1]),
        row_suffix_values.reshape(-1, row_suffix_values.shape[-1]),
    )
    attn, router, up, *pieces = merge_parts(
        arrived, suffix, stats, expert_ids[0], router_weight.T, up_weights, *pieces
    )
    attn = exchange(attn.reshape(heads, DEST_ROWS, HEAD_SIZE), "head")
    parts, chosen, residual_lines = project(
        attn.reshape(heads * DEST_ROWS, HEAD_SIZE), pieces
    )
    groups = [[y * near + n for n in range(near)] for y in range(SPREAD)]
    parts = exchange(parts, "head", groups)
    x = exchange(sum_parts(parts, residual_lines, heads), "head")
    made, hidden = run_experts(
        x, chosen, marks, norm_gain[None], router, gate_weights, up, down_weights
    )
    return add_parts(exchange(made, "head"), hidden)[None]


def solution(mesh):
    return jax.shard_map(
        layer,
        mesh=mesh,
        in_specs=(
            P("head", None, None),
            P("head", "grp", None),
            P("head", "grp", None),
            P("head", "grp", None, None),
            P("head", "grp", None, None),
            P("head", "grp"),
            P("head", "grp", None),
            P("head", None),
            P(),
            P(),
            P("head", None, None),
            P("head", None, None),
            P("head", None, None),
            P("head", "grp", None),
        ),
        out_specs=P("head", "grp", None),
        check_vma=False,
    )
```

```python
import math

import jax
import jax.numpy as jnp
from jax import lax
from jax.experimental import pallas as pl
from jax.experimental.pallas import tpu as pltpu
from jax.sharding import PartitionSpec as P


QUERY_HEADS = 32
KEY_VALUE_HEADS = 4
HEAD_SIZE = 128
GROUP = QUERY_HEADS // KEY_VALUE_HEADS
LANES = 128
STAT_ROWS = 8
DEST_ROWS = 16
SPREAD = 4
EXPERTS_HERE = 2
EXTRA_ROWS = 8

masked_score = -1e30
norm_epsilon = 1e-06
score_scale = 1.0 / math.sqrt(HEAD_SIZE)
f32 = jnp.float32
bf16 = jnp.bfloat16
INTERPRET = False


def exchange(x, axis, groups=None):
    return lax.all_to_all(
        x, axis, split_axis=0, concat_axis=0, tiled=True, axis_index_groups=groups
    )


def kernel_call(body, outs, scratch, *args, hbm=(), hbm_outs=()):
    vmem = pl.BlockSpec(memory_space=pltpu.VMEM)
    raw = pl.BlockSpec(memory_space=pltpu.HBM)
    specs = [raw if i in hbm else vmem for i in range(len(args))]
    args = [
        pltpu.with_memory_space_constraint(a, pltpu.HBM) if i in hbm else a
        for i, a in enumerate(args)
    ]
    return pl.pallas_call(
        body,
        out_shape=outs,
        in_specs=specs,
        out_specs=tuple(raw if i in hbm_outs else vmem for i in range(len(outs))),
        scratch_shapes=scratch,
        compiler_params=pltpu.CompilerParams(vmem_limit_bytes=16 << 20),
        interpret=INTERPRET,
    )(*args)


def shape(dims, dtype):
    return jax.ShapeDtypeStruct(dims, dtype)


def head_columns(k):
    return slice(k * HEAD_SIZE, (k + 1) * HEAD_SIZE)


def dot_last(a, b):
    return lax.dot_general(a, b, (((1,), (1,)), ((), ())), preferred_element_type=f32)


def dot_first(a, b):
    return lax.dot_general(a, b, (((0,), (0,)), ((), ())), preferred_element_type=f32)


def start_copy(source, target, sem):
    copy = pltpu.make_async_copy(source, target, sem)
    copy.start()
    return copy


def prefix_body(
    q_hbm, k_hbm, v_hbm, weight_hbm, residual_hbm, out_hbm, own_ref, mark_ref, *refs
):
    pieces, refs = refs[:SPREAD], refs[SPREAD:]
    q_in, k_in, v_in, q_rows, stats, rests, made, in_sems, out_sems = refs[:9]
    weight, residual, extra, extras, pack_sems = refs[9:]
    rows = q_hbm.shape[0]
    dests = out_hbm.shape[0]
    per_dest = rows * GROUP // dests
    width = rows * GROUP
    wide = GROUP * HEAD_SIZE
    keys = start_copy(k_hbm, k_in, in_sems.at[KEY_VALUE_HEADS])
    arrivals = [
        start_copy(q_hbm.at[:, k * wide : (k + 1) * wide], q_in.at[k], in_sems.at[k])
        for k in range(KEY_VALUE_HEADS)
    ]
    values = start_copy(v_hbm, v_in, in_sems.at[KEY_VALUE_HEADS + 1])
    loads = start_packing(weight_hbm, residual_hbm, weight, residual, pack_sems)
    stats[...] = jnp.zeros(stats.shape, f32)
    rests[...] = jnp.zeros(rests.shape, f32)
    lane = lax.broadcasted_iota(jnp.int32, mark_ref.shape, 1)
    row = lax.broadcasted_iota(jnp.int32, mark_ref.shape, 0)
    first = lax.axis_index("head") * EXPERTS_HERE
    mark_ref[...] = (lane == first + row).astype(f32)
    start = pl.multiple_of(lax.axis_index("grp") * per_dest, per_dest)
    departures = []
    for k in range(KEY_VALUE_HEADS):
        arrivals[k].wait()
        if k == 0:
            keys.wait()
        for j in range(GROUP):
            q_rows[k, pl.ds(j, rows, stride=GROUP), :] = q_in[k, :, head_columns(j)].astype(f32)
        mine = slice(k * per_dest, (k + 1) * per_dest)
        own_ref[mine, :] = q_rows[k, pl.ds(start, per_dest), :]
        scores = dot_last(k_in[:, head_columns(k)], q_rows[k].astype(bf16)) * score_scale
        top = jnp.max(scores, 0, keepdims=True)
        top_high = top.astype(bf16).astype(f32)
        top_low = (top - top_high).astype(bf16).astype(f32)
        terms = jnp.exp(scores - (top_high + top_low))
        mass = jnp.sum(terms, 0, keepdims=True)
        mass_high = mass.astype(bf16).astype(f32)
        stats[k : k + 1, 0:width] = top_high
        stats[4 + k : 5 + k, 0:width] = mass_high
        rests[k : k + 1, 0:width] = top_low
        rests[4 + k : 5 + k, 0:width] = mass - mass_high
        if k == 0:
            values.wait()
        weighted = dot_first(terms.astype(bf16), v_in[:, head_columns(k)])
        made[:, mine, :] = weighted.astype(bf16).reshape(dests, per_dest, HEAD_SIZE)
        departures.append(start_copy(made.at[:, mine, :], out_hbm.at[:, mine, :], out_sems.at[k]))
    held = stats[...]
    rest = pltpu.roll(rests[...], per_dest, 1)
    low = lax.broadcasted_iota(jnp.int32, (STAT_ROWS, LANES), 1) < per_dest
    last = slice(KEY_VALUE_HEADS * per_dest, KEY_VALUE_HEADS * per_dest + STAT_ROWS)
    for d in range(dests):
        at = slice(d * per_dest, d * per_dest + LANES)
        made[d, last, :] = jnp.where(low, held[:, at], rest[:, at]).astype(bf16)
    departures.append(
        start_copy(made.at[:, last, :], out_hbm.at[:, last, :], out_sems.at[KEY_VALUE_HEADS])
    )
    departures += finish_packing(loads, pieces, weight, residual, extra, extras, pack_sems)
    for copy in departures:
        copy.wait()


def place_of(heads):
    return lax.axis_index("head") // (heads // SPREAD)


def start_packing(weight_hbm, residual_hbm, weight, residual, sems):
    load = start_copy(weight_hbm, weight, sems.at[0])
    return load, start_copy(residual_hbm, residual, sems.at[1])


def finish_packing(loads, outs, weight, residual, extra, extras, sems):
    depth, width = weight.shape[0], outs[0].shape[1]
    for load in loads:
        load.wait()
    copies = []
    for s in range(SPREAD):
        start = (place_of(QUERY_HEADS) + s) & (SPREAD - 1)
        start = pl.multiple_of(start * width, width)
        extra[...] = jnp.zeros(extra.shape, f32)
        extra[0:2, :] = residual[:, pl.ds(start, width)].astype(f32)
        extras[s] = extra[...].astype(bf16)
        pairs = (
            (extras.at[s], outs[s].at[depth : depth + EXTRA_ROWS, :]),
            (weight.at[:, pl.ds(start, width)], outs[s].at[0:depth, :]),
        )
        copies += [start_copy(a, b, sems.at[2 + 2 * s + n]) for n, (a, b) in enumerate(pairs)]
    return copies


def window_body(
    own_ref, length_hbm, k_hbm, v_hbm, out_ref, stat_ref, length_ref, k_ref, v_ref, sems
):
    pairs = ((length_hbm, length_ref), (k_hbm, k_ref), (v_hbm, v_ref))
    copies = [start_copy(a, b, sems.at[n]) for n, (a, b) in enumerate(pairs)]
    for copy in copies:
        copy.wait()
    suffix_attention(length_ref, own_ref, k_ref, v_ref, out_ref, stat_ref)


def suffix_attention(length_ref, own_ref, k_ref, v_ref, out_ref, stat_ref):
    per_dest = own_ref.shape[0] // KEY_VALUE_HEADS
    keys = k_ref.shape[0]
    half = keys // 2
    row = lax.broadcasted_iota(jnp.int32, (keys, per_dest), 0)
    lane = lax.broadcasted_iota(jnp.int32, (keys, per_dest), 1)
    second = row >= half
    limit = jnp.where(second, length_ref[:, 1:2] + half, length_ref[:, 0:1])
    inside = (second == (lane >= GROUP)) & (row < limit)
    stat_ref[...] = jnp.zeros(stat_ref.shape, f32)
    for k in range(KEY_VALUE_HEADS):
        q = own_ref[k * per_dest : (k + 1) * per_dest, :].astype(bf16)
        scores = dot_last(k_ref[:, head_columns(k)], q) * score_scale
        scores = jnp.where(inside, scores, masked_score)
        top = jnp.max(scores, 0, keepdims=True)
        terms = jnp.where(inside, jnp.exp(scores - top), 0.0)
        mass = jnp.sum(terms, 0, keepdims=True)
        stat_ref[k : k + 1, 0:per_dest] = top
        stat_ref[4 + k : 5 + k, 0:per_dest] = mass
        out_ref[k * per_dest : (k + 1) * per_dest, :] = dot_first(
            terms.astype(bf16), v_ref[:, head_columns(k)]
        )


def merge_body(
    suffix_ref, stat_ref, part_hbm, id_hbm, router_hbm, up_hbm,
    out_ref, router_ref, up_ref, part_ref, id_ref, rows, heads, sems,
):
    pairs = (
        (part_hbm, part_ref),
        (id_hbm, id_ref),
        (router_hbm, router_ref),
        (up_hbm, up_ref),
    )
    copies = [start_copy(a, b, sems.at[n]) for n, (a, b) in enumerate(pairs)]
    rows[...] = jnp.zeros(rows.shape, f32)
    copies[0].wait()
    sources = part_ref.shape[0]
    per_dest = suffix_ref.shape[0] // KEY_VALUE_HEADS
    first = KEY_VALUE_HEADS * per_dest
    held = [stat_ref[...]]
    for g in range(sources):
        both = part_ref[g, first : first + STAT_ROWS, :].astype(f32)
        held.append(both + pltpu.roll(both, LANES - per_dest, 1))
    top = held[0]
    for t in held[1:]:
        top = jnp.maximum(top, t)
    scales = [jnp.exp(t - top) for t in held]
    masses = [pltpu.roll(t, 4, 0) for t in held]
    total = scales[0] * masses[0]
    for s, m in zip(scales[1:], masses[1:]):
        total = total + s * m
    inverse = 1.0 / total
    scales = [s * inverse for s in scales]
    scales += [jnp.zeros((8, LANES), f32)] * (-len(scales) % 16)
    table = jnp.concatenate(scales, 0)
    turned = jnp.concatenate(
        [table[i : i + LANES].T[0:per_dest] for i in range(0, table.shape[0], LANES)], 1
    )
    for k in range(KEY_VALUE_HEADS):
        mine = slice(k * per_dest, (k + 1) * per_dest)
        mixed = turned[:, k : k + 1] * suffix_ref[mine, :]
        for g in range(sources):
            at = (g + 1) * 8 + k
            mixed = mixed + turned[:, at : at + 1] * part_ref[g, mine, :].astype(f32)
        for i in range(2):
            heads[i * QUERY_HEADS + k * GROUP : i * QUERY_HEADS + (k + 1) * GROUP, :] = mixed[
                i * GROUP : (i + 1) * GROUP
            ]
    near = QUERY_HEADS // SPREAD
    for y in range(SPREAD):
        for s in range(SPREAD):
            source = (y - s) % SPREAD * near
            for i in range(2):
                at = y * near * DEST_ROWS + i * SPREAD + s
                rows[pl.ds(at, near, stride=DEST_ROWS), :] = heads[
                    i * QUERY_HEADS + source : i * QUERY_HEADS + source + near, :
                ]
    copies[1].wait()
    lane = lax.broadcasted_iota(jnp.int32, (QUERY_HEADS, LANES), 1)
    for i in range(2):
        chosen = lane == id_ref[i : i + 1, 0:1]
        for n in range(1, id_ref.shape[1]):
            chosen = chosen | (lane == id_ref[i : i + 1, n : n + 1])
        line = chosen.astype(f32)
        rows[pl.ds(2 * SPREAD + i, QUERY_HEADS, stride=DEST_ROWS), :] = line
    out_ref[...] = rows[...].astype(bf16)
    for copy in copies[2:]:
        copy.wait()


def project_body(attn_ref, *refs):
    pieces, (out_ref, chosen_ref, residual_ref, rows, lines) = refs[:SPREAD], refs[SPREAD:]
    count = attn_ref.shape[0] // DEST_ROWS
    depth = pieces[0].shape[0] - EXTRA_ROWS
    near = count // SPREAD
    blocks = pieces[0].shape[1] // LANES
    rows[...] = attn_ref[...].astype(f32)
    for i in range(2):
        line = rows[pl.ds(2 * SPREAD + i, count, stride=DEST_ROWS), :]
        chosen_ref[i * count : (i + 1) * count, :] = line
    made = jnp.zeros((2 * count, blocks * LANES), f32)
    for s in range(SPREAD):
        attn = [rows[pl.ds(i * SPREAD + s, count, stride=DEST_ROWS), :] for i in range(2)]
        attn = jnp.concatenate(attn, 0).astype(bf16)
        made = made + jnp.dot(attn, pieces[s][0:depth, :], preferred_element_type=f32)
        extra = pieces[s][depth : depth + EXTRA_ROWS, :].astype(f32)
        source = (place_of(count) + SPREAD - s) & (SPREAD - 1)
        for i in range(2):
            for c in range(blocks):
                residual_ref[pl.ds(c * 2 * SPREAD + i * SPREAD + source, 1), :] = extra[
                    i : i + 1, c * LANES : (c + 1) * LANES
                ]
    for c in range(blocks):
        lines[c] = made[:, c * LANES : (c + 1) * LANES]
    for n in range(near):
        parts = [lines[c, pl.ds(n, 2 * SPREAD, stride=near), :] for c in range(blocks)]
        out_ref[n] = jnp.concatenate(parts, 0).astype(bf16)


def spread_rows(made, lines, count, blocks):
    for i in range(2):
        for c in range(blocks):
            lines[pl.ds(i * blocks + c, count, stride=2 * blocks), :] = made[
                i * count : (i + 1) * count, c * LANES : (c + 1) * LANES
            ]


def sum_body(part_ref, residual_ref, out_ref):
    hidden = residual_ref[...]
    for n in range(part_ref.shape[0]):
        hidden = hidden + part_ref[n].astype(f32)
    hidden = hidden.astype(bf16)
    for h in range(out_ref.shape[0]):
        out_ref[h] = hidden


def expert_body(
    x_ref, chosen_ref, mark_ref, gain_ref, router_ref, gate, up, down_hbm,
    out_ref, hidden_ref, lines, x_rows, down, sems,
):
    experts = gate.shape[0]
    copies = [start_copy(down_hbm.at[e], down.at[e], sems.at[e]) for e in range(experts)]
    count, size, _ = x_ref.shape
    near = count // SPREAD
    pairs = 2 * SPREAD
    blocks = size // pairs
    own = lax.axis_index("head")
    far = own // near
    lines[...] = x_ref[...].astype(f32).reshape(lines.shape)
    for y in range(SPREAD):
        for c in range(blocks):
            for n in range(near):
                at = (y * near + n) * size + c * pairs
                x_rows[y * blocks + c, pl.ds(n, pairs, stride=near), :] = lines[at : at + pairs, :]
            for i in range(2):
                at = (y * near + own - far * near) * size + c * pairs + i * SPREAD + far
                to = (i * SPREAD + y) * blocks + c
                hidden_ref[to : to + 1, :] = lines[pl.ds(at, 1), :]
    hidden = jnp.concatenate([x_rows[c] for c in range(SPREAD * blocks)], 1)
    mean_square = jnp.sum(hidden * hidden, 1, keepdims=True) / hidden.shape[1]
    x = (hidden * lax.rsqrt(mean_square + norm_epsilon) * gain_ref[...]).astype(bf16)
    logits = dot_last(x, router_ref[...])
    expo = jnp.where(chosen_ref[:, 0 : logits.shape[1]] > 0.5, jnp.exp(logits), 0.0)
    mass = jnp.sum(expo, 1, keepdims=True)
    mixed = jnp.zeros((2 * count, down.shape[2]), f32)
    for e in range(experts):
        gate_out = jnp.dot(x, gate[e], preferred_element_type=f32)
        up_out = jnp.dot(x, up[e], preferred_element_type=f32)
        act = (gate_out / (1.0 + jnp.exp(-gate_out)) * up_out).astype(bf16)
        copies[e].wait()
        made = jnp.dot(act, down[e], preferred_element_type=f32).astype(bf16).astype(f32)
        mark = mark_ref[e : e + 1, 0 : expo.shape[1]] > 0.5
        mine = jnp.sum(jnp.where(mark, expo, 0.0), 1, keepdims=True)
        mixed = mixed + (mine / mass) * made
    spread_rows(mixed, lines, count, size // 2)
    out_ref[...] = lines[...].astype(bf16).reshape(count, size, LANES)


def final_body(part_ref, hidden_ref, out_ref, lines):
    sources, size, _ = part_ref.shape
    blocks = size // 2
    total = part_ref[0].astype(f32)
    for s in range(1, sources):
        total = total + part_ref[s].astype(f32)
    lines[...] = hidden_ref[...] + total
    for c in range(blocks):
        out_ref[:, c * LANES : (c + 1) * LANES] = lines[pl.ds(c, 2, stride=blocks), :]


def prefix_attention(q, k, v, weight, residual, dests):
    rows = q.shape[0]
    per_dest = rows * GROUP // dests
    send = (dests, KEY_VALUE_HEADS * per_dest + STAT_ROWS, HEAD_SIZE)
    padded = (rows * GROUP // LANES + 1) * LANES
    piece = (weight.shape[0] + EXTRA_ROWS, weight.shape[1] // SPREAD)
    made, own, marks, *pieces = kernel_call(
        prefix_body,
        (
            pltpu.HBM(send, bf16),
            shape((KEY_VALUE_HEADS * per_dest, HEAD_SIZE), f32),
            shape((8, LANES), f32),
            *(pltpu.HBM(piece, bf16) for _ in range(SPREAD)),
        ),
        [
            pltpu.VMEM((KEY_VALUE_HEADS, rows, GROUP * HEAD_SIZE), bf16),
            pltpu.VMEM(k.shape, bf16),
            pltpu.VMEM(v.shape, bf16),
            pltpu.VMEM((KEY_VALUE_HEADS, rows * GROUP, HEAD_SIZE), f32),
            pltpu.VMEM((STAT_ROWS, padded), f32),
            pltpu.VMEM((STAT_ROWS, padded), f32),
            pltpu.VMEM(send, bf16),
            pltpu.SemaphoreType.DMA((KEY_VALUE_HEADS + 2,)),
            pltpu.SemaphoreType.DMA((KEY_VALUE_HEADS + 1,)),
            pltpu.VMEM(weight.shape, bf16),
            pltpu.VMEM(residual.shape, bf16),
            pltpu.VMEM((EXTRA_ROWS, piece[1]), f32),
            pltpu.VMEM((SPREAD, EXTRA_ROWS, piece[1]), bf16),
            pltpu.SemaphoreType.DMA((2 + 2 * SPREAD,)),
        ],
        q, k, v, weight, residual, hbm=range(5), hbm_outs=(0, *range(3, 3 + SPREAD)),
    )
    return made, own, marks, pieces


def fill_window(lengths, own, k, v):
    return kernel_call(
        window_body,
        (shape(own.shape, f32), shape((STAT_ROWS, LANES), f32)),
        [
            pltpu.VMEM(lengths.shape, jnp.int32),
            pltpu.VMEM(k.shape, bf16),
            pltpu.VMEM(v.shape, bf16),
            pltpu.SemaphoreType.DMA((3,)),
        ],
        own, lengths, k, v, hbm=(1, 2, 3),
    )


def merge_parts(suffix, stats, parts, ids, *weights):
    dims = (QUERY_HEADS * DEST_ROWS, HEAD_SIZE)
    return kernel_call(
        merge_body,
        (shape(dims, bf16), *(shape(w.shape, bf16) for w in weights)),
        [
            pltpu.VMEM(parts.shape, bf16),
            pltpu.VMEM(ids.shape, jnp.int32),
            pltpu.VMEM(dims, f32),
            pltpu.VMEM((2 * QUERY_HEADS, HEAD_SIZE), f32),
            pltpu.SemaphoreType.DMA((2 + len(weights),)),
        ],
        suffix, stats, parts, ids, *weights, hbm=range(2, 4 + len(weights)),
    )


def project(attn, pieces):
    count = attn.shape[0] // DEST_ROWS
    near, blocks = count // SPREAD, pieces[0].shape[1] // LANES
    size = 2 * SPREAD * blocks
    return kernel_call(
        project_body,
        (
            shape((near, size, LANES), bf16),
            shape((2 * count, LANES), f32),
            shape((size, LANES), f32),
        ),
        [pltpu.VMEM(attn.shape, f32), pltpu.VMEM((blocks, 2 * count, LANES), f32)],
        attn, *pieces,
    )


def sum_parts(parts, residual, heads):
    return kernel_call(
        sum_body, (shape((heads, *parts.shape[1:]), bf16),), [], parts, residual
    )[0]


def run_experts(x, chosen, marks, gain, router, gate, up, down):
    count, size, _ = x.shape
    return kernel_call(
        expert_body,
        (shape(x.shape, bf16), shape((size, LANES), f32)),
        [
            pltpu.VMEM((count * size, LANES), f32),
            pltpu.VMEM((size // 2, 2 * count, LANES), f32),
            pltpu.VMEM(down.shape, bf16),
            pltpu.SemaphoreType.DMA((down.shape[0],)),
        ],
        x, chosen, marks, gain, router, gate, up, down, hbm=(7,),
    )


def add_parts(parts, hidden):
    size = parts.shape[1]
    return kernel_call(
        final_body,
        (shape((2, size // 2 * LANES), f32),),
        [pltpu.VMEM((size, LANES), f32)],
        parts, hidden,
    )[0]


def layer(
    queries,
    shared_prefix_keys,
    shared_prefix_values,
    row_suffix_keys,
    row_suffix_values,
    suffix_lengths,
    residual,
    out_weight,
    norm_gain,
    router_weight,
    gate_weights,
    up_weights,
    down_weights,
    expert_ids,
):
    heads = lax.axis_size("head")
    dests = lax.axis_size("grp")
    send, own, marks, pieces = prefix_attention(
        queries[0],
        shared_prefix_keys[0],
        shared_prefix_values[0],
        out_weight,
        residual[0],
        dests,
    )
    arrived = exchange(send, "grp")
    near = heads // SPREAD
    for s in range(1, SPREAD):
        ring = [(h, (h + s * near) % heads) for h in range(heads)]
        pieces[s] = lax.ppermute(pieces[s], "head", ring)
        pieces[s] = pltpu.with_memory_space_constraint(pieces[s], pltpu.HBM)
    suffix, stats = fill_window(
        suffix_lengths,
        own,
        row_suffix_keys.reshape(-1, row_suffix_keys.shape[-1]),
        row_suffix_values.reshape(-1, row_suffix_values.shape[-1]),
    )
    attn, router, up = merge_parts(
        suffix, stats, arrived, expert_ids[0], router_weight.T, up_weights
    )
    attn = exchange(attn.reshape(heads, DEST_ROWS, HEAD_SIZE), "head")
    parts, chosen, residual_lines = project(
        attn.reshape(heads * DEST_ROWS, HEAD_SIZE), pieces
    )
    groups = [[y * near + n for n in range(near)] for y in range(SPREAD)]
    parts = exchange(parts, "head", groups)
    x = exchange(sum_parts(parts, residual_lines, heads), "head")
    made, hidden = run_experts(
        x, chosen, marks, norm_gain[None], router, gate_weights, up, down_weights
    )
    return add_parts(exchange(made, "head"), hidden)[None]


def solution(mesh):
    return jax.shard_map(
        layer,
        mesh=mesh,
        in_specs=(
            P("head", None, None),
            P("head", "grp", None),
            P("head", "grp", None),
            P("head", "grp", None, None),
            P("head", "grp", None, None),
            P("head", "grp"),
            P("head", "grp", None),
            P("head", None),
            P(),
            P(),
            P("head", None, None),
            P("head", None, None),
            P("head", None, None),
            P("head", "grp", None),
        ),
        out_specs=P("head", "grp", None),
        check_vma=False,
    )
```
